256 devices in a mesh: dp: 2 (over core), graph: 128 (over x, z, y).
Axes of the slice: x: 4, y: 4, z: 8, core: 2. Of those that a mesh axis runs over, the one named last changes fastest.
Arguments:
- features: bfloat16 [4096, 49, 128], P(('dp', 'graph')), may hold values from -6 to 6
- cotangent: bfloat16 [4096, 49, 128], P(('dp', 'graph')), may hold values from -0.029907227 to 0.029907227
- wigner: bfloat16 [256, 29, 49], replicated, may hold values from -2 to 2
- src_atom: int32 [32768], P(('dp', 'graph')), may hold values from 0 to 15
- dst_part: int32 [32768, 1], P(('dp', 'graph')), may hold values from 0 to 127; in each aligned block of 128 rows (0 to 127, 128 to 255, ...) at most 2 rows name the same one
- dst_atom: int32 [32768], P(('dp', 'graph')), may hold values from 0 to 15
- angle: int32 [32768], P(('dp', 'graph')), may hold values from 0 to 255
- w_zero: bfloat16 [896, 896], replicated, may hold values from -0.1875 to 0.1875
- w_one: bfloat16 [2, 768, 768], replicated, may hold values from -0.15625 to 0.15625
- w_two: bfloat16 [2, 640, 640], replicated, may hold values from -0.15625 to 0.15625
Outputs:
- aggregated: bfloat16 [4096, 49, 128], P(('dp', 'graph'))
- weight_grad: float32 [2801664], P('graph')
The draws below stay inside these ranges and needn't reach their ends.
Inputs may be any that keep to these rules, and one draw needn't show every extreme that they name: `dst_part`: the edges of one device go to at most 2 per partition; in every draw some device sends exactly 2 edges to some partition.
All inputs are finite; a program needn't handle non-finite values.
Results may differ from the reference program's by a relative error of at most 0.0057.
Values may be sent and summed in bfloat16 or wider, within the bound.
A program may use at most 128 MiB of HBM per device.

```python
import math
import jax
import jax.numpy as jnp
import numpy as np
from jax import lax

LMAX = 6
MMAX = 2
CHANNELS = 128
ATOM_DEV = 16
ANGLES = 256
COEFFS = 49
KEPT = 29
PARAMS = 2801664
EDGE_DEV = 128
CAP = 2
ATOMS = 4096
EDGES = 32768
N_GRAPH = 128


def with_ends(values, own_key, low, high):
    index_at = [jax.random.randint(jax.random.fold_in(own_key, axis), (), 0, length) for axis, length in enumerate(values.shape)]
    main_axis = values.shape.index(max(values.shape))
    beside = index_at[:main_axis] + [(index_at[main_axis] + 1) % values.shape[main_axis]] + index_at[main_axis + 1:]
    return values.at[tuple(index_at)].set(low).at[tuple(beside)].set(high)


def level_of(rng, extent, cuts, low, high):
    gain = 1.0
    for dim, parts in cuts:
        steps = jax.random.uniform(jax.random.fold_in(jax.random.fold_in(rng, 6), dim), (parts,), jnp.float32, low / len(cuts), high / len(cuts))
        gain = gain * jnp.repeat(jnp.exp(steps), extent[dim] // parts).reshape((-1,) + (1,) * (len(extent) - 1 - dim))
    return gain


def shared_out(own_key, own, number, rows, count, top, limit, lean):
    order = jax.random.permutation(own_key, count)
    crowded, ordinary = load_shares(count, rows * top, limit, lean, True), load_shares(count, rows * top, limit, lean, False)
    places = jnp.arange(count)

    def named(sizes, offset_by):
        used = int((sizes > 0).sum())
        fixed = max(1, used // 4)
        passed = fixed + (places - fixed + offset_by * (used - fixed)) % max(1, count - fixed)
        return jnp.zeros((count,), jnp.int32).at[order[jnp.where(places < fixed, places, passed)]].set(jnp.asarray(sizes, jnp.int32))

    sizes = jnp.where(number % 4 == 0, named(crowded, number // 4), named(ordinary, number - number // 4 - 1))
    mixed = jax.random.permutation(jax.random.fold_in(own, 3), count)
    giver, receiver = mixed[0:count // 2 * 2:2], mixed[1:count // 2 * 2:2]
    margin = jnp.minimum(sizes[giver] - 1, limit - sizes[receiver]) // 2
    margin = jnp.where((giver == order[0]) | (receiver == order[0]) | (sizes[receiver] == 0), 0, jnp.maximum(margin, 0))
    passed = jax.random.randint(jax.random.fold_in(own, 4), (count // 2,), 0, 1 << 20) % (margin + 1)
    sizes = sizes.at[giver].add(-passed).at[receiver].add(passed)
    items = jnp.searchsorted(jnp.cumsum(sizes), jnp.arange(rows * top), side="right").astype(jnp.int32)
    grid = items.reshape(top, rows).T
    grid = grid[jax.random.permutation(jax.random.fold_in(own, 1), rows)]
    offset_by = jax.random.randint(jax.random.fold_in(own, 2), (rows, 1), 0, top)
    return jnp.take_along_axis(grid, (jnp.arange(top)[None, :] + offset_by) % top, axis=1)


def load_shares(amount, total, reach, skew, full):
    weights = [(1 << 20) // math.isqrt(rank ** skew) + 1 for rank in range(1, amount + 1)]
    largest = reach if full else min(reach, max(-(-total // amount), total * weights[0] // sum(weights)))
    least = 1 if total - largest >= amount - 1 else 0
    given, rest = [largest] + [least] * (amount - 1), total - largest - least * (amount - 1)
    while rest > 0:
        free = [i for i in range(1, amount) if given[i] < largest] or [i for i in range(1, amount) if given[i] < reach]
        pool, left = sum([weights[i] for i in free]), rest
        for i in free:
            extra = min(reach - given[i], max(1, left * weights[i] // pool), rest)
            given[i] = given[i] + extra
            rest = rest - extra
    return np.array(given)


def normal_values(own_key, extent, width, limit, split=(), kind=jnp.bfloat16):
    entries = width * jax.random.normal(own_key, extent, jnp.float32)
    if split:
        entries = entries * level_of(own_key, extent, split, -0.22, 0.18)
    return jnp.clip(entries, -limit, limit).astype(kind)


def setup_inputs(seed: int = 0) -> dict:
    key_list = jax.random.split(jax.random.key(seed), 11)
    features = normal_values(key_list[0], (ATOMS, COEFFS, CHANNELS), 1.0, 6.0, ((0, 256),))
    cotangent = normal_values(key_list[1], (ATOMS, COEFFS, CHANNELS), 0.005, 0.029907227, ((0, 256),))
    wigner = normal_values(key_list[2], (ANGLES, KEPT, COEFFS), 0.35, 2.0)
    src_atom = with_ends(jax.random.randint(key_list[3], (EDGES,), 0, ATOM_DEV), jax.random.fold_in(key_list[3], 1), 0, ATOM_DEV - 1).astype(jnp.int32)
    dst_part_keys = jax.random.split(jax.random.fold_in(key_list[4], 1), EDGES // EDGE_DEV)
    dst_part_turns = jax.random.permutation(jax.random.fold_in(key_list[4], 3), EDGES // EDGE_DEV)
    dst_part = jax.vmap(lambda own, number: shared_out(jax.random.fold_in(key_list[4], 2), own, number, EDGE_DEV, N_GRAPH, 1, CAP, 2))(dst_part_keys, dst_part_turns).reshape((EDGES, 1))
    dst_atom = with_ends(jax.random.randint(key_list[5], (EDGES,), 0, ATOM_DEV), jax.random.fold_in(key_list[5], 1), 0, ATOM_DEV - 1).astype(jnp.int32)
    angle = with_ends(jax.random.randint(key_list[6], (EDGES,), 0, ANGLES), jax.random.fold_in(key_list[6], 1), 0, ANGLES - 1).astype(jnp.int32)
    w_zero = normal_values(key_list[7], ((LMAX + 1) * CHANNELS, (LMAX + 1) * CHANNELS), ((LMAX + 1) * CHANNELS) ** -0.5, 0.1875)
    w_one = normal_values(key_list[8], (2, LMAX * CHANNELS, LMAX * CHANNELS), (2 * LMAX * CHANNELS) ** -0.5, 0.15625)
    w_two = normal_values(key_list[9], (2, (LMAX - 1) * CHANNELS, (LMAX - 1) * CHANNELS), (2 * (LMAX - 1) * CHANNELS) ** -0.5, 0.15625)
    return {"features": features, "cotangent": cotangent, "wigner": wigner, "src_atom": src_atom, "dst_part": dst_part, "dst_atom": dst_atom, "angle": angle, "w_zero": w_zero, "w_one": w_one, "w_two": w_two}


def kept_pairs():
    listing = []
    for azimuth in range(MMAX + 1):
        sign_list = [1] if azimuth == 0 else [1, -1]
        for sign_of in sign_list:
            for degree in range(azimuth, LMAX + 1):
                listing.append((degree, sign_of * azimuth))
    return listing


def degree_mask():
    full_degrees = np.repeat(np.arange(LMAX + 1), 2 * np.arange(LMAX + 1) + 1)
    kept_degrees = np.array([degree_pair[0] for degree_pair in kept_pairs()])
    return (kept_degrees[:, None] == full_degrees[None, :]).astype(np.float32)


def group_bounds():
    bounds = [(0, LMAX + 1)]
    offset = LMAX + 1
    for azimuth in range(1, MMAX + 1):
        length = LMAX + 1 - azimuth
        bounds.append((offset, length))
        bounds.append((offset + length, length))
        offset = offset + 2 * length
    return bounds


def flat_group(tile_rows, first_row, length):
    return tile_rows[:, first_row:first_row + length].reshape(tile_rows.shape[0], length * tile_rows.shape[2])


def so2_mix(tile_rows, weights):
    bounds = group_bounds()
    count_rows = tile_rows.shape[0]
    channel_count = tile_rows.shape[2]
    zero_out = jnp.dot(flat_group(tile_rows, 0, LMAX + 1), weights[0], preferred_element_type=jnp.float32)
    pieces = [zero_out.reshape(count_rows, LMAX + 1, channel_count)]
    for azimuth in range(1, MMAX + 1):
        plus_start, length = bounds[2 * azimuth - 1]
        minus_start = bounds[2 * azimuth][0]
        plus_part = flat_group(tile_rows, plus_start, length)
        minus_part = flat_group(tile_rows, minus_start, length)
        real_w = weights[azimuth][0]
        imag_w = weights[azimuth][1]
        out_plus = jnp.dot(plus_part, real_w, preferred_element_type=jnp.float32) - jnp.dot(minus_part, imag_w, preferred_element_type=jnp.float32)
        out_minus = jnp.dot(plus_part, imag_w, preferred_element_type=jnp.float32) + jnp.dot(minus_part, real_w, preferred_element_type=jnp.float32)
        pieces.append(out_plus.reshape(count_rows, length, channel_count))
        pieces.append(out_minus.reshape(count_rows, length, channel_count))
    return jnp.concatenate(pieces, axis=1).astype(jnp.bfloat16)


def gram_matrix(left_rows, right_rows):
    return lax.dot_general(left_rows, right_rows, (((0,), (0,)), ((), ())), preferred_element_type=jnp.float32)


def so2_grads(tile_rows, grad_rows):
    bounds = group_bounds()
    flat_parts = [gram_matrix(flat_group(tile_rows, 0, LMAX + 1), flat_group(grad_rows, 0, LMAX + 1)).reshape(-1)]
    for azimuth in range(1, MMAX + 1):
        plus_start, length = bounds[2 * azimuth - 1]
        minus_start = bounds[2 * azimuth][0]
        tile_plus = flat_group(tile_rows, plus_start, length)
        tile_minus = flat_group(tile_rows, minus_start, length)
        grad_plus = flat_group(grad_rows, plus_start, length)
        grad_minus = flat_group(grad_rows, minus_start, length)
        real_g = gram_matrix(tile_plus, grad_plus) + gram_matrix(tile_minus, grad_minus)
        imag_g = gram_matrix(tile_plus, grad_minus) - gram_matrix(tile_minus, grad_plus)
        flat_parts.append(jnp.stack([real_g, imag_g]).reshape(-1))
    return jnp.concatenate(flat_parts)


def reference(features, cotangent, wigner, src_atom, dst_part, dst_atom, angle, w_zero, w_one, w_two):
    weights = [w_zero, w_one, w_two]
    wigner_table = wigner.astype(jnp.float32) * jnp.asarray(degree_mask(), dtype=jnp.float32)
    blocks = src_atom.shape[0] // EDGE_DEV
    block_ids = jnp.arange(blocks, dtype=jnp.int32)
    edge_inputs = (block_ids, src_atom.reshape(blocks, EDGE_DEV), dst_part[:, 0].reshape(blocks, EDGE_DEV), dst_atom.reshape(blocks, EDGE_DEV), angle.reshape(blocks, EDGE_DEV))

    def visit_block(carried, inputs):
        summed, grad_sum = carried
        block_id, src_blk, part_blk, dst_blk, angle_blk = inputs
        src_rows = block_id * ATOM_DEV + src_blk
        replica = block_id // N_GRAPH
        dst_rows = (replica * N_GRAPH + part_blk) * ATOM_DEV + dst_blk
        rotation = wigner_table[angle_blk]
        source_x = features[src_rows].astype(jnp.float32)
        rotated = jnp.einsum("ekj,ejc->ekc", rotation, source_x, precision=lax.Precision.HIGHEST).astype(jnp.bfloat16)
        message = so2_mix(rotated, weights)
        returned = jnp.einsum("ekj,ekc->ejc", rotation, message.astype(jnp.float32), precision=lax.Precision.HIGHEST)
        summed = summed.at[dst_rows].add(returned)
        upstream = cotangent[dst_rows].astype(jnp.float32)
        pulled = jnp.einsum("ekj,ejc->ekc", rotation, upstream, precision=lax.Precision.HIGHEST).astype(jnp.bfloat16)
        grad_sum = grad_sum + so2_grads(rotated, pulled)
        return (summed, grad_sum), None

    start_sum = jnp.zeros(features.shape, jnp.float32)
    start_grad = jnp.zeros((PARAMS,), jnp.float32)
    (summed, grad_sum), unused = lax.scan(visit_block, (start_sum, start_grad), edge_inputs)
    return summed.astype(jnp.bfloat16), grad_sum
```

```python
import functools

import jax
import jax.numpy as jnp
from jax import lax
from jax.experimental import pallas as pl
from jax.experimental.pallas import tpu as pltpu
from jax.sharding import PartitionSpec as P

LMAX = 6
MMAX = 2
NX, NZ, NY = 4, 8, 4
NXY = NX * NY
EDGES = 128
ATOMS = 16
SLOTS = 256
ROWS = 21888
SHARD = 171
QUART = 48
MESH = pl.DeviceIdType.MESH
BF = jnp.bfloat16
F32 = jnp.float32


def kept_degrees():
    out = list(range(LMAX + 1))
    for m in range(1, MMAX + 1):
        for _ in range(2):
            out.extend(range(m, LMAX + 1))
    return out


DEGREE = kept_degrees()
KEPT = len(DEGREE)
WIRE = KEPT + 2
GROUPS = [(0, 7), (7, 6), (13, 6), (19, 5), (24, 5)]


def width(degree):
    return 128 if degree <= 3 else 256


def dot(a, b):
    return jnp.dot(a, b, preferred_element_type=F32)


def iota(shape, dim):
    return lax.broadcasted_iota(jnp.int32, shape, dim)


def remote(src, dst, send, recv, device):
    return pltpu.make_async_remote_copy(
        src_ref=src, dst_ref=dst, send_sem=send, recv_sem=recv, device_id=device, device_id_type=MESH
    )


def build_table(wig, table):
    for degree in range(LMAX + 1):
        w = width(degree)
        j = iota((128, w), 0)
        n = iota((128, w), 1)
        spread = ((j == degree * degree + n // ATOMS) & (n < ATOMS * (2 * degree + 1))).astype(BF)
        for k in [k for k in range(KEPT) if DEGREE[k] == degree]:
            table[k, :, 0:w] = dot(wig[k], spread).astype(BF)


def build_rotation(angle, atom, table, left):
    lane = iota((SLOTS, 128), 1)
    near = (angle == lane.astype(F32)).astype(BF)
    far = (angle == (lane + 128).astype(F32)).astype(BF)
    pick = jnp.concatenate([near, far], axis=1)
    mask = (atom == (lane % ATOMS + 1).astype(F32)).astype(F32)
    wide = jnp.concatenate([mask, mask], axis=1)
    for k in range(KEPT):
        w = width(DEGREE[k])
        gate = mask if w == 128 else wide
        left[k, :, 0:w] = (dot(pick, table[k, :, 0:w]) * gate).astype(BF)


def kernel(
    tgt, src, dat, ang, wig, feat, cot, w0, w1, w2,
    agg, wgrad,
    table, left, mycode, codes, fall, cpad, sendb, recvb, pull, xt, flat,
    pk, r0, sa, sb, ra, ta, rb, rc, sa1, sb1, ra1, ta1, rb1, rc1, sa2, sb2, r3, fin,
    code_s, code_r, ring_s, ring_r, ex_s, ex_r, loc_s, dp_s, dp_r, st_s, st_r, z_s, z_r, f_s, f_r,
):
    dp = lax.axis_index("dp")
    g = lax.axis_index("graph")
    x = g // 32
    z = (g // 4) % 8
    y = g % 4
    xy = x * 4 + y

    def at(px, pz, py):
        return (dp, px * 32 + pz * 4 + py)

    partner = (1 - dp, g)

    def zpeer(i):
        return lax.rem(z + i, NZ)

    def xypeer(i):
        return lax.rem(xy + i, NXY)

    barrier = pltpu.get_barrier_semaphore()

    def greet_z(i, c):
        pl.semaphore_signal(barrier, inc=1, device_id=at(x, zpeer(i), y), device_id_type=MESH)
        return c

    def greet_xy(i, c):
        q = xypeer(i)
        pl.semaphore_signal(barrier, inc=1, device_id=at(q // 4, z, q % 4), device_id_type=MESH)
        return c

    lax.fori_loop(1, NZ, greet_z, 0)
    lax.fori_loop(1, NXY, greet_xy, 0)
    pl.semaphore_signal(barrier, inc=1, device_id=partner, device_id_type=MESH)

    trow = jnp.broadcast_to(tgt[...], (EDGES, EDGES)).astype(F32)
    tcol = jnp.transpose(trow)
    earlier = (tcol == trow) & (iota((EDGES, EDGES), 0) < iota((EDGES, EDGES), 1))
    rank = jnp.sum(earlier.astype(F32), axis=0, keepdims=True).astype(jnp.int32)
    t = tgt[...]
    pos = ((t >> 2) & 7) * 32 + ((t >> 5) * 4 + (t & 3)) * 2 + rank
    hot = (iota((SLOTS, EDGES), 0) == jnp.broadcast_to(pos, (SLOTS, EDGES))).astype(BF)
    for i, row in enumerate([ang[...], src[...] + 1, dat[...] + 1]):
        wide = jnp.broadcast_to(row, (EDGES, EDGES)).astype(F32).astype(BF)
        got = lax.dot_general(hot, wide, (((1,), (1,)), ((), ())), preferred_element_type=F32)
        mycode[:, i] = got.astype(BF).reshape(NZ, 32, 128)

    fall[z, 0:784] = feat[...]
    for q in range(NZ):
        fall[q, 784:832] = jnp.zeros((48, 128), BF)
    pl.semaphore_wait(barrier, 23)

    sign = 1 - 2 * dp

    def ring(step_sem, block, direction):
        dev = at(x, lax.rem(z + direction + NZ, NZ), y)
        part = fall.at[block, pl.ds(0, 784)]
        return remote(part, part, ring_s.at[step_sem], ring_r.at[step_sem], dev)

    def behind(n):
        return lax.rem(z - sign * n + 2 * NZ, NZ)

    def ahead(n):
        return lax.rem(z + sign * n + 2 * NZ, NZ)

    ring(0, z, sign).start()
    ring(4, z, -sign).start()

    def code_copy(i):
        q = zpeer(i)
        return remote(mycode.at[q], codes.at[z], code_s.at[i], code_r.at[i], at(x, q, y))

    def send_code(i, c):
        code_copy(i).start()
        return c

    def wait_code(i, c):
        code_copy(i).wait()
        return c

    lax.fori_loop(1, NZ, send_code, 0)
    codes[z] = mycode[z]
    build_table(wig, table)
    lax.fori_loop(1, NZ, wait_code, 0)
    build_rotation(
        codes[:, 0].reshape(SLOTS, 128).astype(F32), codes[:, 1].reshape(SLOTS, 128).astype(F32), table, left
    )

    def exchange(step, zz, i):
        q = xypeer(i)
        return remote(
            sendb.at[step, :, q], recvb.at[:, zz, xy], ex_s.at[step, i], ex_r.at[step, i], at(q // 4, z, q % 4)
        )

    def own_copy(step, zz):
        return pltpu.make_async_copy(sendb.at[step, :, xy], recvb.at[:, zz, xy], loc_s.at[step])

    def rotate(step, zz):
        rows = pl.ds(pl.multiple_of(zz * 32, 32), 32)
        for degree in range(LMAX + 1):
            w = width(degree)
            ks = [k for k in range(KEPT) if DEGREE[k] == degree]
            lhs = jnp.concatenate([left[k, rows, 0:w] for k in ks], axis=0)
            lo = ATOMS * degree * degree
            got = dot(lhs, fall[zz, lo : lo + w]).astype(BF)
            for i, k in enumerate(ks):
                sendb[step, k] = got[32 * i : 32 * i + 32].reshape(NXY, 2, 128)
        sendb[step, KEPT] = codes[zz, 0].reshape(NXY, 2, 128)
        sendb[step, KEPT + 1] = codes[zz, 2].reshape(NXY, 2, 128)

        def go(i, c):
            exchange(step, zz, i).start()
            return c

        lax.fori_loop(1, NXY, go, 0)
        own_copy(step, zz).start()

    order = [z]
    for n in range(1, 5):
        order.append(behind(n))
        if n < 4:
            order.append(ahead(n))
    for step in range(NZ):
        n = (step + 1) // 2
        if step % 2 == 1:
            ring(n - 1, behind(n), sign).wait_recv()
            if n < 4:
                ring(n, behind(n), sign).start()
        elif step:
            ring(3 + n, ahead(n), -sign).wait_recv()
            if n < 3:
                ring(4 + n, ahead(n), -sign).start()
        rotate(step, order[step])
    for n in range(4):
        ring(n, z, sign).wait_send()
    for n in range(3):
        ring(4 + n, z, -sign).wait_send()

    for step in range(NZ):

        def done(i, c):
            exchange(step, order[step], i).wait()
            return c

        lax.fori_loop(1, NXY, done, 0)
        own_copy(step, order[step]).wait()

    def rot(k):
        return recvb[k].reshape(SLOTS, 128)

    build_rotation(rot(KEPT).astype(F32), rot(KEPT + 1).astype(F32), table, left)
    cpad[0:784] = cot[...]
    cpad[784:832] = jnp.zeros((48, 128), BF)
    for k in range(KEPT):
        w = width(DEGREE[k])
        lo = ATOMS * DEGREE[k] * DEGREE[k]
        pull[k] = dot(left[k, :, 0:w], cpad[lo : lo + w]).astype(BF)
        xt[k] = jnp.transpose(rot(k).astype(F32)).astype(BF)

    def cat(ks):
        return jnp.concatenate([rot(k) for k in ks], axis=1)

    message = {}
    zero = dot(cat(range(7)), w0[...]).astype(BF)
    for i in range(7):
        message[i] = zero[:, 128 * i : 128 * i + 128]
    for m, w in ((1, w1), (2, w2)):
        plus, length = GROUPS[2 * m - 1]
        minus = GROUPS[2 * m][0]
        p, q = cat(range(plus, plus + length)), cat(range(minus, minus + length))
        up = (dot(p, w[0]) - dot(q, w[1])).astype(BF)
        um = (dot(p, w[1]) + dot(q, w[0])).astype(BF)
        for i in range(length):
            message[plus + i] = up[:, 128 * i : 128 * i + 128]
            message[minus + i] = um[:, 128 * i : 128 * i + 128]
    for degree in range(LMAX + 1):
        w = width(degree)
        ks = [k for k in range(KEPT) if DEGREE[k] == degree]
        lhs = jnp.concatenate([left[k, :, 0:w] for k in ks], axis=0)
        rhs = jnp.concatenate([message[k] for k in ks], axis=0)
        got = lax.dot_general(lhs, rhs, (((0,), (0,)), ((), ())), preferred_element_type=F32)
        size = 2 * degree + 1
        agg[degree * degree : (degree + 1) * (degree + 1)] = (
            got[0 : ATOMS * size].astype(BF).reshape(size, ATOMS, 128)
        )

    def spread(res, base, length, lo, width_):
        for jb in range(lo, lo + width_):
            flat[pl.ds(base + jb, 128 * length, stride=length), :] = res[:, 128 * (jb - lo) : 128 * (jb - lo) + 128]

    zt = jnp.concatenate([xt[k] for k in range(7)], axis=0)
    for lo in range(0, 7, 2):
        n = min(2, 7 - lo)
        rhs = jnp.concatenate([pull[lo + i] for i in range(n)], axis=1)
        spread(dot(zt, rhs), 0, 7, lo, n)
    base = 896 * 7
    for m in (1, 2):
        plus, length = GROUPS[2 * m - 1]
        minus = GROUPS[2 * m][0]
        pqt = jnp.concatenate(
            [jnp.concatenate([xt[plus + i], xt[minus + i]], axis=1) for i in range(length)], axis=0
        )
        for lo in range(0, length, 2):
            n = min(2, length - lo)
            gg = jnp.concatenate([pull[plus + lo + i] for i in range(n)], axis=1)
            hh = jnp.concatenate([pull[minus + lo + i] for i in range(n)], axis=1)
            spread(dot(pqt, jnp.concatenate([gg, hh], axis=0)), base, length, lo, n)
            spread(dot(pqt, jnp.concatenate([hh, -gg], axis=0)), base + 128 * length * length, length, lo, n)
        base += 2 * 128 * length * length
    flat[ROWS : ROWS + 24] = jnp.zeros((24, 128), F32)

    def pack(s, c):
        for a in range(2):
            pk[a, s] = flat[pl.ds(SHARD * s + QUART * (2 * (1 - dp) + a), QUART), :].astype(BF)
        return c

    lax.fori_loop(0, 128, pack, 0)
    swap = remote(pk, r0, dp_s, dp_r, partner)
    swap.start()
    swap.wait()

    def merge(s, c):
        sx = s // 32
        sz = (s // 4) % 8
        sy = s % 4
        sa[sx, sy, sz] = (flat[pl.ds(SHARD * s + QUART * 2 * dp, QUART), :] + r0[0, s].astype(F32)).astype(BF)
        sb[sy, sx, sz] = (flat[pl.ds(SHARD * s + QUART * (2 * dp + 1), QUART), :] + r0[1, s].astype(F32)).astype(BF)
        return c

    lax.fori_loop(0, 128, merge, 0)

    def along_x(d):
        return at(lax.rem(x + d + NX, NX), z, y)

    def along_y(d):
        return at(x, z, lax.rem(y + d + NY, NY))

    def stage(number, parts):
        chains = []
        for i, (p, move, s, r_a, t_a, r_b, r_c, out) in enumerate(parts):

            def chunk(d, s=s, p=p):
                return s.at[lax.rem(p + d + 4, 4)]

            first = remote(chunk(2 * sign), r_a, st_s.at[number, i, 0], st_r.at[number, i, 0], move(sign))
            second = remote(chunk(-sign), r_b, st_s.at[number, i, 1], st_r.at[number, i, 1], move(-sign))
            third = remote(t_a, r_c, st_s.at[number, i, 2], st_r.at[number, i, 2], move(sign))
            first.start()
            second.start()
            chains.append((first, second, third, chunk))
        for (p, move, s, r_a, t_a, r_b, r_c, out), (first, second, third, chunk) in zip(parts, chains):
            first.wait_recv()
            t_a[...] = (r_a[...].astype(F32) + chunk(sign)[...].astype(F32)).astype(BF)
            third.start()
        for (p, move, s, r_a, t_a, r_b, r_c, out), (first, second, third, chunk) in zip(parts, chains):
            second.wait_recv()
            third.wait_recv()
            out[...] = (chunk(0)[...].astype(F32) + r_b[...].astype(F32) + r_c[...].astype(F32)).astype(BF)
            first.wait_send()
            second.wait_send()
            third.wait_send()

    stage(
        0,
        [
            (x, along_x, sa, ra.at[0], ta.at[0], rb.at[0], rc.at[0], sa1),
            (y, along_y, sb, ra.at[1], ta.at[1], rb.at[1], rc.at[1], sb1),
        ],
    )
    stage(
        1,
        [
            (y, along_y, sa1, ra1.at[0], ta1.at[0], rb1.at[0], rc1.at[0], sa2),
            (x, along_x, sb1, ra1.at[1], ta1.at[1], rb1.at[1], rc1.at[1], sb2),
        ],
    )

    for a, s2 in ((0, sa2), (1, sb2)):

        def zcopy(i, s2=s2, a=a):
            q = zpeer(i)
            return remote(s2.at[q], r3.at[a, i], z_s.at[a, i], z_r.at[a, i], at(x, q, y))

        def zgo(i, c):
            zcopy(i).start()
            return c

        lax.fori_loop(1, NZ, zgo, 0)
    for a, s2 in ((0, sa2), (1, sb2)):
        total = s2[z].astype(F32)
        for i in range(1, NZ):
            remote(s2.at[zpeer(i)], r3.at[a, i], z_s.at[a, i], z_r.at[a, i], at(x, zpeer(i), y)).wait()
            total = total + r3[a, i].astype(F32)
        fin[2 * dp + a] = total
    last = remote(fin.at[pl.ds(2 * dp, 2)], fin.at[pl.ds(2 * dp, 2)], f_s, f_r, partner)
    last.start()
    last.wait()
    for q in range(4):
        n = min(QUART, SHARD - QUART * q)
        wgrad[QUART * q : QUART * q + n] = fin[q, 0:n]


def shards(features, cotangent, wigner, src_atom, dst_part, dst_atom, angle, w_zero, w_one, w_two):
    feat = jnp.transpose(features, (1, 0, 2)).reshape(784, 128)
    cot = jnp.transpose(cotangent, (1, 0, 2)).reshape(784, 128)
    wig = jnp.pad(jnp.transpose(wigner, (1, 0, 2)), ((0, 0), (0, 0), (0, 128 - 49)))
    dma = pltpu.SemaphoreType.DMA
    chunk = (32, QUART, 128)
    scratch = [
        pltpu.VMEM((KEPT, SLOTS, 256), BF),
        pltpu.VMEM((KEPT, SLOTS, 256), BF),
        pltpu.VMEM((NZ, 3, 32, 128), BF),
        pltpu.VMEM((NZ, 3, 32, 128), BF),
        pltpu.VMEM((NZ, 832, 128), BF),
        pltpu.VMEM((832, 128), BF),
        pltpu.VMEM((NZ, WIRE, NXY, 2, 128), BF),
        pltpu.VMEM((WIRE, NZ, NXY, 2, 128), BF),
        pltpu.VMEM((KEPT, SLOTS, 128), BF),
        pltpu.VMEM((KEPT, 128, SLOTS), BF),
        pltpu.VMEM((ROWS + 24, 128), F32),
        pltpu.VMEM((2, 128, QUART, 128), BF),
        pltpu.VMEM((2, 128, QUART, 128), BF),
        pltpu.VMEM((NX, NY, NZ, QUART, 128), BF),
        pltpu.VMEM((NY, NX, NZ, QUART, 128), BF),
    ]
    for lead in ((4, NZ), (NZ,)):
        scratch += [pltpu.VMEM((2,) + lead + (QUART, 128), BF) for _ in range(4)]
        scratch += [pltpu.VMEM(lead + (QUART, 128), BF) for _ in range(2)]
    scratch += [
        pltpu.VMEM((2, NZ, QUART, 128), BF),
        pltpu.VMEM((4, QUART, 128), F32),
        dma((NZ,)), dma((NZ,)),
        dma((7,)), dma((7,)),
        dma((NZ, NXY)), dma((NZ, NXY)), dma((NZ,)),
        dma, dma,
        dma((2, 2, 3)), dma((2, 2, 3)),
        dma((2, NZ)), dma((2, NZ)),
        dma, dma,
    ]
    vmem = pl.BlockSpec(memory_space=pltpu.VMEM)
    agg, wgrad = pl.pallas_call(
        kernel,
        out_shape=(
            jax.ShapeDtypeStruct((49, ATOMS, 128), BF),
            jax.ShapeDtypeStruct((SHARD, 128), F32),
        ),
        in_specs=[vmem] * 10,
        out_specs=(vmem, vmem),
        scratch_shapes=scratch,
        compiler_params=pltpu.CompilerParams(
            collective_id=0, has_side_effects=True, vmem_limit_bytes=67000000
        ),
    )(
        dst_part.reshape(1, EDGES),
        src_atom.reshape(1, EDGES),
        dst_atom.reshape(1, EDGES),
        angle.reshape(1, EDGES),
        wig, feat, cot, w_zero, w_one, w_two,
    )
    return jnp.transpose(agg, (1, 0, 2)), wgrad.reshape(SHARD * 128)


def solution(mesh):
    both = ("dp", "graph")
    placed = (
        P(both, None, None), P(both, None, None), P(), P(both), P(both, None), P(both), P(both), P(), P(), P(),
    )
    return jax.shard_map(
        shards,
        mesh=mesh,
        in_specs=placed,
        out_specs=(P(both, None, None), P("graph")),
        check_vma=False,
    )
```

```python
import functools

import jax
import jax.numpy as jnp
from jax import lax
from jax.experimental import pallas as pl
from jax.experimental.pallas import tpu as pltpu
from jax.sharding import PartitionSpec as P

LMAX = 6
MMAX = 2
NX, NZ, NY = 4, 8, 4
NXY = NX * NY
EDGES = 128
ATOMS = 16
SLOTS = 256
ROWS = 21888
SHARD = 171
HALF = 88
RING = 32
REST = 24
MESH = pl.DeviceIdType.MESH
BF = jnp.bfloat16
F32 = jnp.float32


def kept_degrees():
    out = list(range(LMAX + 1))
    for m in range(1, MMAX + 1):
        for _ in range(2):
            out.extend(range(m, LMAX + 1))
    return out


DEGREE = kept_degrees()
KEPT = len(DEGREE)
WIRE = KEPT + 2
SPLIT = 21
CODE = SPLIT - 2
BY_DEGREE = sorted(range(KEPT), key=lambda k: (DEGREE[k], k))
PLACE = {k: i if i < CODE else i + 2 for i, k in enumerate(BY_DEGREE)}
GROUPS = [(0, 7), (7, 6), (13, 6), (19, 5), (24, 5)]


def width(degree):
    return 128 if degree <= 3 else 256


def dot(a, b):
    return jnp.dot(a, b, preferred_element_type=F32)


def iota(shape, dim):
    return lax.broadcasted_iota(jnp.int32, shape, dim)


def remote(src, dst, send, recv, device):
    return pltpu.make_async_remote_copy(
        src_ref=src, dst_ref=dst, send_sem=send, recv_sem=recv, device_id=device, device_id_type=MESH
    )


def build_table(wig, wk, table):
    wk[...] = jnp.zeros_like(wk)
    wk[:, 0:49, :] = jnp.swapaxes(wig[...].astype(F32), 0, 1).astype(BF)
    for degree in range(LMAX + 1):
        w = width(degree)
        j = iota((w, 64), 1)
        n = iota((w, 64), 0)
        spread = ((j == degree * degree + n // ATOMS) & (n < ATOMS * (2 * degree + 1))).astype(BF)
        for k in [k for k in range(KEPT) if DEGREE[k] == degree]:
            table[k, 0:w] = dot(spread, wk[k]).astype(BF)


def build_rotation(angle, atom, table, left, rows):
    size = angle.shape[0]
    lane = iota((size, 128), 1)
    near = (angle == lane.astype(F32)).astype(BF)
    far = (angle == (lane + 128).astype(F32)).astype(BF)
    pick = jnp.concatenate([near, far], axis=1)
    mask = (atom == (lane % ATOMS + 1).astype(F32)).astype(F32)
    wide = jnp.concatenate([mask, mask], axis=1)
    for k in range(KEPT):
        w = width(DEGREE[k])
        gate = mask if w == 128 else wide
        got = lax.dot_general(pick, table[k, 0:w], (((1,), (1,)), ((), ())), preferred_element_type=F32)
        got = (got * gate).astype(BF)
        step = size // len(rows)
        for i, part in enumerate(rows):
            left[k, part, 0:w] = got[step * i : step * i + step]


def kernel(
    tgt, src, dat, ang, wig_in, feat, cot, w0_in, w1_in, w2_in,
    agg, wgrad,
    wig, w0, w1, w2, table, wk, left, leftd, crow, codes, fall, cpad, sendb, recvb, pull, xt, flat,
    pk, r0, s0, ra, ta, rb, rc, s1, ra1, ta1, rb1, rc1, s2, r3, fin,
    sz, ua, va, ub, vb, sz1, r4,
    code_s, code_r, ring_s, ring_r, ex_s, ex_r, loc_s, dp_s, dp_r, st_s, st_r, su_s, su_r, z_s, z_r, f_s, f_r, in_s,
    ua_s, ua_r, ub_s, ub_r, w_s, w_r,
):
    dp = lax.axis_index("dp")
    g = lax.axis_index("graph")
    x = g // 32
    z = (g // 4) % 8
    y = g % 4
    xy = x * 4 + y
    sign = 1 - 2 * dp

    def at(px, pz, py):
        return (dp, px * 32 + pz * 4 + py)

    partner = (1 - dp, g)

    def zpeer(i):
        return lax.rem(z + i, NZ)

    def xypeer(i):
        return lax.rem(xy + i, NXY)

    barrier = pltpu.get_barrier_semaphore()

    def greet_z(i, c):
        pl.semaphore_signal(barrier, inc=1, device_id=at(x, zpeer(i), y), device_id_type=MESH)
        return c

    def greet_xy(i, c):
        q = xypeer(i)
        pl.semaphore_signal(barrier, inc=1, device_id=at(q // 4, z, q % 4), device_id_type=MESH)
        return c

    lax.fori_loop(1, NZ, greet_z, 0)
    lax.fori_loop(1, NXY, greet_xy, 0)
    pl.semaphore_signal(barrier, inc=1, device_id=partner, device_id_type=MESH)

    loads = [
        pltpu.make_async_copy(a, b, in_s.at[i])
        for i, (a, b) in enumerate(
            [
                (wig_in, wig), (feat, fall.at[z, pl.ds(0, 784)]), (cot, cpad.at[pl.ds(0, 784)]),
                (w0_in, w0), (w1_in, w1), (w2_in, w2),
            ]
        )
    ]
    for load in loads:
        load.start()

    trow = jnp.broadcast_to(tgt[...], (EDGES, EDGES)).astype(F32)
    tcol = jnp.transpose(trow)
    earlier = (tcol == trow) & (iota((EDGES, EDGES), 0) < iota((EDGES, EDGES), 1))
    rank = jnp.sum(earlier.astype(F32), axis=0, keepdims=True).astype(jnp.int32)
    t = tgt[...]
    pos = ((t >> 2) & 7) * 32 + ((t >> 5) * 4 + (t & 3)) * 2 + rank
    line = iota((16, EDGES), 0)
    code = jnp.zeros((16, EDGES), jnp.int32)
    for i, row in enumerate([pos, ang[...], src[...] + 1, dat[...] + 1]):
        code = jnp.where(line == i, jnp.broadcast_to(row, (16, EDGES)), code)
    crow[z] = code.astype(F32).astype(BF)

    def expand(q):
        c = crow[q].astype(F32)
        hot = (iota((32, EDGES), 0) + 32 * z).astype(F32) == jnp.broadcast_to(c[0:1], (32, EDGES))
        wide = jnp.concatenate([jnp.broadcast_to(c[i : i + 1], (EDGES, EDGES)) for i in (1, 2, 3)], axis=0)
        got = lax.dot_general(
            hot.astype(BF), wide.astype(BF), (((1,), (1,)), ((), ())), preferred_element_type=F32
        )
        for i in range(3):
            codes[q, i] = got[:, 128 * i : 128 * i + 128].astype(BF)

    for q in range(NZ):
        fall[q, 784:832] = jnp.zeros((48, 128), BF)
    loads[0].wait()
    build_table(wig, wk, table)
    expand(z)
    mine = pl.ds(pl.multiple_of(z * 32, 32), 32)
    build_rotation(codes[z, 0].astype(F32), codes[z, 1].astype(F32), table, left, [mine])

    def exchange(step, piece, i):
        q = xypeer(i)
        part = pl.ds(0, SPLIT) if piece == 0 else pl.ds(SPLIT, WIRE - SPLIT)
        return remote(
            sendb.at[step, part, q], recvb.at[part, step, xy], ex_s.at[step], ex_r.at[step], at(q // 4, z, q % 4)
        )

    def own_copy(step):
        return pltpu.make_async_copy(sendb.at[step, :, xy], recvb.at[:, step, xy], loc_s.at[step])

    def rotate(step, piece, zz):
        rows = pl.ds(pl.multiple_of(zz * 32, 32), 32)
        for degree in range(5) if piece == 0 else range(5, LMAX + 1):
            w = width(degree)
            ks = [k for k in range(KEPT) if DEGREE[k] == degree]
            lhs = jnp.concatenate([left[k, rows, 0:w] for k in ks], axis=0)
            lo = ATOMS * degree * degree
            if piece == 0:
                w = min(w, 400 - lo)
                lhs = lhs[:, 0:w]
            got = dot(lhs, fall[zz, lo : lo + w]).astype(BF)
            for i, k in enumerate(ks):
                sendb[step, PLACE[k]] = got[32 * i : 32 * i + 32].reshape(NXY, 2, 128)
        if piece == 0:
            sendb[step, CODE] = codes[zz, 0].reshape(NXY, 2, 128)
            sendb[step, CODE + 1] = codes[zz, 2].reshape(NXY, 2, 128)

    def send_block(step, piece):
        def go(i, c):
            exchange(step, piece, i).start()
            return c

        lax.fori_loop(1, NXY, go, 0)
        if piece:
            own_copy(step).start()

    def whole(step):
        part = recvb.at[:, step, pl.ds(0, NXY - 1)]
        return remote(part, part, ex_s.at[step], ex_r.at[step], at(x, z, y))

    def receive_block(step):
        whole(step).wait_recv()
        own_copy(step).wait()

    loads[1].wait()
    rotate(0, 0, z)
    rotate(0, 1, z)
    pl.semaphore_wait(barrier, 23)

    def code_copy(i):
        return remote(crow.at[z], crow.at[z], code_s.at[i], code_r.at[i], at(x, zpeer(i), y))

    def code_in(i):
        q = lax.rem(z - i + NZ, NZ)
        return remote(crow.at[q], crow.at[q], code_s.at[i], code_r.at[i], at(x, zpeer(i), y))

    def send_code(i, c):
        code_copy(i).start()
        return c

    def wait_code(i, c):
        code_in(i).wait_recv()
        return c

    def sent_code(i, c):
        code_copy(i).wait_send()
        return c

    lax.fori_loop(1, NZ, send_code, 0)

    def ring(hop, piece, block, direction):
        dev = at(x, lax.rem(z + direction + NZ, NZ), y)
        part = fall.at[block, pl.ds(400 * piece, 400 - 16 * piece)]
        return remote(part, part, ring_s.at[hop, piece], ring_r.at[hop, piece], dev)

    def behind(n):
        return lax.rem(z - sign * n + 2 * NZ, NZ)

    def ahead(n):
        return lax.rem(z + sign * n + 2 * NZ, NZ)

    for piece in range(2):
        ring(0, piece, z, sign).start()
    send_block(0, 0)
    send_block(0, 1)
    cpad[784:832] = jnp.zeros((48, 128), BF)

    def prepare(blocks):
        for q in blocks:
            expand(q)
        rows = [pl.ds(pl.multiple_of(q * 32, 32), 32) for q in blocks]
        build_rotation(
            jnp.concatenate([codes[q, 0] for q in blocks], axis=0).astype(F32),
            jnp.concatenate([codes[q, 1] for q in blocks], axis=0).astype(F32),
            table, left, rows,
        )

    def half(h):
        rows = pl.ds(128 * h, 128)

        def rot(k):
            return recvb[k, 4 * h : 4 * h + 4].reshape(128, 128)

        build_rotation(rot(CODE).astype(F32), rot(CODE + 1).astype(F32), table, leftd, [rows])
        for k in range(KEPT):
            w = width(DEGREE[k])
            lo = ATOMS * DEGREE[k] * DEGREE[k]
            pull[k, rows] = dot(leftd[k, rows, 0:w], cpad[lo : lo + w]).astype(BF)
            xt[k, :, rows] = jnp.transpose(rot(PLACE[k]).astype(F32)).astype(BF)

    def pass_on(n, piece, back):
        if back:
            ring(n - 1, piece, behind(n), sign).wait_recv()
            if n < 4:
                ring(n, piece, behind(n), sign).start()
        elif n < 4:
            ring(3 + n, piece, ahead(n), -sign).wait_recv()
            if n < 3:
                ring(4 + n, piece, ahead(n), -sign).start()

    code_in(1).wait_recv()
    code_in(NZ - 1).wait_recv()
    prepare([behind(1), ahead(1)])
    for piece in range(2):
        ring(4, piece, z, -sign).start()
    for n in range(1, 5):
        for back in (True, False):
            if n == 4 and not back:
                break
            step = 2 * n - 1 if back else 2 * n
            for piece in range(2):
                pass_on(n, piece, back)
                if n == 2 and back and piece == 0:
                    lax.fori_loop(2, NZ - 1, wait_code, 0)
                    prepare([behind(2), ahead(2), behind(3), ahead(3), behind(4)])
                rotate(step, piece, behind(n) if back else ahead(n))
                send_block(step, piece)
    loads[2].wait()
    for early in range(4):
        receive_block(early)
    half(0)
    for late in range(4, NZ):
        receive_block(late)
    half(1)

    def spread(res, base, length, lo, width_):
        for jb in range(lo, lo + width_):
            flat[pl.ds(base + jb, 128 * length, stride=length), :] = res[:, 128 * (jb - lo) : 128 * (jb - lo) + 128]

    def grads(m):
        if m == 0:
            zt = jnp.concatenate([xt[k] for k in range(7)], axis=0)
            for lo in range(0, 7, 2):
                n = min(2, 7 - lo)
                rhs = jnp.concatenate([pull[lo + i] for i in range(n)], axis=1)
                spread(dot(zt, rhs), 0, 7, lo, n)
            return
        base = 128 * (49 if m == 1 else 49 + 72)
        plus, length = GROUPS[2 * m - 1]
        minus = GROUPS[2 * m][0]
        pqt = jnp.concatenate(
            [jnp.concatenate([xt[plus + i], xt[minus + i]], axis=1) for i in range(length)], axis=0
        )
        for lo in range(0, length, 2):
            n = min(2, length - lo)
            gg = jnp.concatenate([pull[plus + lo + i] for i in range(n)], axis=1)
            hh = jnp.concatenate([pull[minus + lo + i] for i in range(n)], axis=1)
            spread(dot(pqt, jnp.concatenate([gg, hh], axis=0)), base, length, lo, n)
            spread(dot(pqt, jnp.concatenate([hh, -gg], axis=0)), base + 128 * length * length, length, lo, n)

    def pack(s, c):
        pk[s] = flat[pl.ds(SHARD * s + HALF * (1 - dp), HALF), :].astype(BF)
        return c

    def merge(s, c):
        sx = s // 32
        cz = (s // 4) % 8
        sy = s % 4
        both = (flat[pl.ds(SHARD * s + HALF * dp, HALF), :] + r0[s].astype(F32)).astype(BF)
        s0[0, sx, sy, cz] = both[0:RING]
        s0[1, sy, sx, cz] = both[RING : 2 * RING]
        sz[cz, sx * 4 + sy] = both[2 * RING : HALF]
        return c

    flat[ROWS : ROWS + 24] = jnp.zeros((24, 128), F32)
    runs = [(0, 36), (36, 90), (90, 128)]
    swaps = []
    for m, (lo, hi) in enumerate(runs):
        grads(m)
        lax.fori_loop(lo, hi, pack, 0)
        part = pl.ds(lo, hi - lo)
        swaps.append(remote(pk.at[part], r0.at[part], dp_s.at[m], dp_r.at[m], partner))
        swaps[m].start()
    for m, (lo, hi) in enumerate(runs):
        swaps[m].wait()
        lax.fori_loop(lo, hi, merge, 0)

    def mixed(k):
        return recvb[k].reshape(SLOTS, 128)

    def cat(ks):
        return jnp.concatenate([mixed(PLACE[k]) for k in ks], axis=1)

    message = {}

    def mix(m):
        if m == 0:
            zero = dot(cat(range(7)), w0[...]).astype(BF)
            for i in range(7):
                message[i] = zero[:, 128 * i : 128 * i + 128]
            return
        w = w1 if m == 1 else w2
        plus, length = GROUPS[2 * m - 1]
        minus = GROUPS[2 * m][0]
        p, q = cat(range(plus, plus + length)), cat(range(minus, minus + length))
        up = (dot(p, w[0]) - dot(q, w[1])).astype(BF)
        um = (dot(p, w[1]) + dot(q, w[0])).astype(BF)
        for i in range(length):
            message[plus + i] = up[:, 128 * i : 128 * i + 128]
            message[minus + i] = um[:, 128 * i : 128 * i + 128]

    def gather_atoms():
        for degree in range(LMAX + 1):
            w = width(degree)
            ks = [k for k in range(KEPT) if DEGREE[k] == degree]
            lhs = jnp.concatenate([leftd[k, :, 0:w] for k in ks], axis=0)
            rhs = jnp.concatenate([message[k] for k in ks], axis=0)
            got = lax.dot_general(lhs, rhs, (((0,), (0,)), ((), ())), preferred_element_type=F32)
            size = 2 * degree + 1
            agg[degree * degree : (degree + 1) * (degree + 1)] = (
                got[0 : ATOMS * size].astype(BF).reshape(size, ATOMS, 128)
            )

    def along_x(d):
        return at(lax.rem(x + d + NX, NX), z, y)

    def along_y(d):
        return at(x, z, lax.rem(y + d + NY, NY))

    def mod4(v):
        return lax.rem(v + 4, 4)

    parts = [(0, x, along_x, y, along_y), (1, y, along_y, x, along_x)]
    one, two, three, subs = [], [], [], []
    for i, p, move, q, _ in parts:
        order = [mod4(q + 2 * sign), mod4(q - sign), mod4(q + sign), q]
        subs.append(order)
        one.append(
            [remote(s0.at[i, mod4(p + 2 * sign), j], ra.at[i, j], st_s.at[i, 0, n], st_r.at[i, 0, n], move(sign))
             for n, j in enumerate(order)]
        )
        two.append(
            [remote(s0.at[i, mod4(p - sign), j], rb.at[i, j], st_s.at[i, 1, n], st_r.at[i, 1, n], move(-sign))
             for n, j in enumerate(order)]
        )
        three.append(
            [remote(ta.at[i, j], rc.at[i, j], st_s.at[i, 2, n], st_r.at[i, 2, n], move(sign))
             for n, j in enumerate(order)]
        )
    def mod8(v):
        return lax.rem(v + 8, 8)

    def up(h, j):
        src = sz.at[mod8(z + 4 * sign), pl.ds(8 * j, 8)] if h == 0 else va.at[h - 1, j]
        return remote(src, ua.at[h, j], ua_s.at[h, j], ua_r.at[h, j], at(x, mod8(z + sign), y))

    def down(h, j):
        src = sz.at[mod8(z - 3 * sign), pl.ds(8 * j, 8)] if h == 0 else vb.at[h - 1, j]
        return remote(src, ub.at[h, j], ub_s.at[h, j], ub_r.at[h, j], at(x, mod8(z - sign), y))

    def pass_sum(h, j):
        part = pl.ds(8 * j, 8)
        up(h, j).wait_recv()
        va[h, j] = (ua[h, j].astype(F32) + sz[mod8(z + (3 - h) * sign), part].astype(F32)).astype(BF)
        up(h + 1, j).start()
        if h < 2:
            down(h, j).wait_recv()
            vb[h, j] = (ub[h, j].astype(F32) + sz[mod8(z - (2 - h) * sign), part].astype(F32)).astype(BF)
            down(h + 1, j).start()

    def end_sum(j):
        part = pl.ds(8 * j, 8)
        up(3, j).wait_recv()
        down(2, j).wait_recv()
        sz1[part] = (sz[z, part].astype(F32) + ua[3, j].astype(F32) + ub[2, j].astype(F32)).astype(BF)

    def relay(n):
        for i, p, *_ in parts:
            j = subs[i][n]
            one[i][n].wait_recv()
            ta[i, j] = (ra[i, j].astype(F32) + s0[i, mod4(p + sign), j].astype(F32)).astype(BF)
            three[i][n].start()

    four, five, six = [], [], []
    for i, p, _, q, move in parts:
        order = subs[i]
        four.append(remote(s1.at[i, order[0]], ra1.at[i], su_s.at[i, 0], su_r.at[i, 0], move(sign)))
        five.append(remote(s1.at[i, order[1]], rb1.at[i], su_s.at[i, 1], su_r.at[i, 1], move(-sign)))
        six.append(remote(ta1.at[i], rc1.at[i], su_s.at[i, 2], su_r.at[i, 2], move(sign)))

    def close(n):
        for i, p, *_ in parts:
            j = subs[i][n]
            two[i][n].wait_recv()
            three[i][n].wait_recv()
            s1[i, j] = (s0[i, p, j].astype(F32) + rb[i, j].astype(F32) + rc[i, j].astype(F32)).astype(BF)
            if n == 0:
                four[i].start()
            if n == 1:
                five[i].start()

    for j in range(2):
        up(0, j).start()
        down(0, j).start()
    for n in range(4):
        for i in range(2):
            one[i][n].start()
            two[i][n].start()
    for load in loads[3:]:
        load.wait()
    mix(1)
    pass_sum(0, 0)
    relay(0)
    pass_sum(0, 1)
    relay(1)
    mix(0)
    pass_sum(1, 0)
    relay(2)
    pass_sum(1, 1)
    relay(3)
    mix(2)
    pass_sum(2, 0)
    close(0)
    pass_sum(2, 1)
    for n in range(1, 4):
        close(n)
    for i in range(2):
        four[i].wait_recv()
        ta1[i] = (ra1[i].astype(F32) + s1[i, subs[i][2]].astype(F32)).astype(BF)
        six[i].start()
    for j in range(2):
        end_sum(j)

    def across(i):
        q = xypeer(i)
        return remote(sz1.at[q], r4.at[i], w_s.at[i], w_r.at[i], at(q // 4, z, q % 4))

    def across_go(i, c):
        across(i).start()
        return c

    lax.fori_loop(1, NXY, across_go, 0)
    gather_atoms()
    for i in range(2):
        five[i].wait_recv()
        six[i].wait_recv()
        s2[i] = (s1[i, subs[i][3]].astype(F32) + rb1[i].astype(F32) + rc1[i].astype(F32)).astype(BF)

    def zcopy(a, i):
        q = zpeer(i)
        return remote(s2.at[a, q], r3.at[a, i], z_s.at[a, i], z_r.at[a, i], at(x, q, y))

    for a in range(2):

        def zgo(i, c):
            zcopy(a, i).start()
            return c

        lax.fori_loop(1, NZ, zgo, 0)
    total = sz1[xy].astype(F32)
    for i in range(1, NXY):
        across(i).wait()
        total = total + r4[i].astype(F32)
    fin[dp, 2 * RING : HALF] = total
    for a in range(2):
        total = s2[a, z].astype(F32)
        for i in range(1, NZ):
            zcopy(a, i).wait()
            total = total + r3[a, i].astype(F32)
        fin[dp, RING * a : RING * a + RING] = total
    last = remote(fin.at[dp], fin.at[dp], f_s, f_r, partner)
    last.start()
    for j in range(2):
        for h in range(4):
            up(h, j).wait_send()
        for h in range(3):
            down(h, j).wait_send()
    for n in range(4):
        for i in range(2):
            one[i][n].wait_send()
            two[i][n].wait_send()
            three[i][n].wait_send()
    for i in range(2):
        four[i].wait_send()
        five[i].wait_send()
        six[i].wait_send()
    for piece in range(2):
        for n in range(4):
            ring(n, piece, z, sign).wait_send()
        for n in range(3):
            ring(4 + n, piece, z, -sign).wait_send()
    for step in range(NZ):
        whole(step).wait_send()
    lax.fori_loop(1, NZ, sent_code, 0)
    last.wait()
    wgrad[0:HALF] = fin[0]
    wgrad[HALF:SHARD] = fin[1, 0 : SHARD - HALF]


def shards(features, cotangent, wigner, src_atom, dst_part, dst_atom, angle, w_zero, w_one, w_two):
    dma = pltpu.SemaphoreType.DMA
    scratch = [
        pltpu.VMEM((49, KEPT, 256), BF),
        pltpu.VMEM(w_zero.shape, BF),
        pltpu.VMEM(w_one.shape, BF),
        pltpu.VMEM(w_two.shape, BF),
        pltpu.VMEM((KEPT, SLOTS, 256), BF),
        pltpu.VMEM((KEPT, 64, 256), BF),
        pltpu.VMEM((KEPT, SLOTS, 256), BF),
        pltpu.VMEM((KEPT, SLOTS, 256), BF),
        pltpu.VMEM((NZ, 16, 128), BF),
        pltpu.VMEM((NZ, 3, 32, 128), BF),
        pltpu.VMEM((NZ, 832, 128), BF),
        pltpu.VMEM((832, 128), BF),
        pltpu.VMEM((NZ, WIRE, NXY, 2, 128), BF),
        pltpu.VMEM((WIRE, NZ, NXY, 2, 128), BF),
        pltpu.VMEM((KEPT, SLOTS, 128), BF),
        pltpu.VMEM((KEPT, 128, SLOTS), BF),
        pltpu.VMEM((ROWS + 24, 128), F32),
        pltpu.VMEM((128, HALF, 128), BF),
        pltpu.VMEM((128, HALF, 128), BF),
        pltpu.VMEM((2, 4, 4, NZ, RING, 128), BF),
    ]
    scratch += [pltpu.VMEM((2, 4, NZ, RING, 128), BF) for _ in range(4)]
    scratch += [pltpu.VMEM((2, 4, NZ, RING, 128), BF)]
    scratch += [pltpu.VMEM((2, NZ, RING, 128), BF) for _ in range(4)]
    scratch += [pltpu.VMEM((2, NZ, RING, 128), BF)]
    scratch += [
        pltpu.VMEM((2, NZ, RING, 128), BF),
        pltpu.VMEM((2, HALF, 128), F32),
        pltpu.VMEM((NZ, NXY, REST, 128), BF),
        pltpu.VMEM((4, 2, 8, REST, 128), BF),
        pltpu.VMEM((3, 2, 8, REST, 128), BF),
        pltpu.VMEM((3, 2, 8, REST, 128), BF),
        pltpu.VMEM((2, 2, 8, REST, 128), BF),
        pltpu.VMEM((NXY, REST, 128), BF),
        pltpu.VMEM((NXY, REST, 128), BF),
        dma((NZ,)), dma((NZ,)),
        dma((7, 2)), dma((7, 2)),
        dma((NZ,)), dma((NZ,)), dma((NZ,)),
        dma((3,)), dma((3,)),
        dma((2, 3, 4)), dma((2, 3, 4)),
        dma((2, 3)), dma((2, 3)),
        dma((2, NZ)), dma((2, NZ)),
        dma, dma,
        dma((6,)),
        dma((4, 2)), dma((4, 2)), dma((3, 2)), dma((3, 2)), dma((NXY,)), dma((NXY,)),
    ]
    vmem = pl.BlockSpec(memory_space=pltpu.VMEM)
    agg, wgrad = pl.pallas_call(
        kernel,
        out_shape=(
            jax.ShapeDtypeStruct((49, ATOMS, 128), BF),
            jax.ShapeDtypeStruct((SHARD, 128), F32),
        ),
        in_specs=[vmem] * 4 + [pl.BlockSpec(memory_space=pl.ANY)] * 6,
        out_specs=(vmem, vmem),
        scratch_shapes=scratch,
        compiler_params=pltpu.CompilerParams(
            collective_id=0, has_side_effects=True, vmem_limit_bytes=67000000
        ),
    )(
        dst_part.reshape(1, EDGES),
        src_atom.reshape(1, EDGES),
        dst_atom.reshape(1, EDGES),
        angle.reshape(1, EDGES),
        jnp.transpose(wigner, (2, 1, 0)),
        jnp.transpose(features, (1, 0, 2)).reshape(784, 128),
        jnp.transpose(cotangent, (1, 0, 2)).reshape(784, 128),
        w_zero, w_one, w_two,
    )
    return jnp.transpose(agg, (1, 0, 2)), wgrad.reshape(SHARD * 128)


def solution(mesh):
    both = ("dp", "graph")
    placed = (
        P(both, None, None), P(both, None, None), P(), P(both), P(both, None), P(both), P(both), P(), P(), P(),
    )
    return jax.shard_map(
        shards,
        mesh=mesh,
        in_specs=placed,
        out_specs=(P(both, None, None), P("graph")),
        check_vma=False,
    )
```

```python
import functools

import jax
import jax.numpy as jnp
from jax import lax
from jax.experimental import pallas as pl
from jax.experimental.pallas import tpu as pltpu
from jax.sharding import PartitionSpec as P

LMAX = 6
MMAX = 2
NX, NZ, NY = 4, 8, 4
NXY = NX * NY
EDGES = 128
ATOMS = 16
SLOTS = 256
ROWS = 21888
SHARD = 171
HALF = 88
RING = 32
REST = 24
MESH = pl.DeviceIdType.MESH
BF = jnp.bfloat16
F32 = jnp.float32


def kept_degrees():
    out = list(range(LMAX + 1))
    for m in range(1, MMAX + 1):
        for _ in range(2):
            out.extend(range(m, LMAX + 1))
    return out


DEGREE = kept_degrees()
KEPT = len(DEGREE)
WIRE = KEPT + 2
SPLIT = 21
CODE = SPLIT - 2
BY_DEGREE = sorted(range(KEPT), key=lambda k: (DEGREE[k], k))
PLACE = {k: i if i < CODE else i + 2 for i, k in enumerate(BY_DEGREE)}
GROUPS = [(0, 7), (7, 6), (13, 6), (19, 5), (24, 5)]


def width(degree):
    return 128 if degree <= 3 else 256


def dot(a, b):
    return jnp.dot(a, b, preferred_element_type=F32)


def iota(shape, dim):
    return lax.broadcasted_iota(jnp.int32, shape, dim)


def remote(src, dst, send, recv, device):
    return pltpu.make_async_remote_copy(
        src_ref=src, dst_ref=dst, send_sem=send, recv_sem=recv, device_id=device, device_id_type=MESH
    )


def build_table(wig, wk, table):
    wk[...] = jnp.zeros_like(wk)
    wk[:, 0:49, :] = jnp.swapaxes(wig[...].astype(F32), 0, 1).astype(BF)
    for degree in range(LMAX + 1):
        w = width(degree)
        j = iota((w, 64), 1)
        n = iota((w, 64), 0)
        spread = ((j == degree * degree + n // ATOMS) & (n < ATOMS * (2 * degree + 1))).astype(BF)
        for k in [k for k in range(KEPT) if DEGREE[k] == degree]:
            table[k, 0:w] = dot(spread, wk[k]).astype(BF)


def build_rotation(angle, atom, table, left, rows):
    size = angle.shape[0]
    lane = iota((size, 128), 1)
    near = (angle == lane.astype(F32)).astype(BF)
    far = (angle == (lane + 128).astype(F32)).astype(BF)
    pick = jnp.concatenate([near, far], axis=1)
    mask = (atom == (lane % ATOMS + 1).astype(F32)).astype(F32)
    wide = jnp.concatenate([mask, mask], axis=1)
    for k in range(KEPT):
        w = width(DEGREE[k])
        gate = mask if w == 128 else wide
        got = lax.dot_general(pick, table[k, 0:w], (((1,), (1,)), ((), ())), preferred_element_type=F32)
        got = (got * gate).astype(BF)
        step = size // len(rows)
        for i, part in enumerate(rows):
            left[k, part, 0:w] = got[step * i : step * i + step]


def kernel(
    tgt, src, dat, ang, wig_in, feat, cot, w0_in, w1_in, w2_in,
    agg_out, wgrad,
    agg, wig, w0, w1, w2, table, wk, left, leftd, crow, codes, fall, cpad, sendb, recvb, pull, xt, flat,
    pk, r0, s0, ra, ta, rb, rc, s1, ra1, ta1, rb1, rc1, s2, r3, fin,
    sz, ua, va, ub, vb, sz1, r4,
    code_s, code_r, ring_s, ring_r, ex_s, ex_r, loc_s, dp_s, dp_r, st_s, st_r, su_s, su_r, z_s, z_r, f_s, f_r, in_s, out_s,
    ua_s, ua_r, ub_s, ub_r, w_s, w_r,
):
    dp = lax.axis_index("dp")
    g = lax.axis_index("graph")
    x = g // 32
    z = (g // 4) % 8
    y = g % 4
    xy = x * 4 + y
    sign = 1 - 2 * dp

    def at(px, pz, py):
        return (dp, px * 32 + pz * 4 + py)

    partner = (1 - dp, g)

    def zpeer(i):
        return lax.rem(z + i, NZ)

    def xypeer(i):
        return lax.rem(xy + i, NXY)

    barrier = pltpu.get_barrier_semaphore()

    def greet_z(i, c):
        pl.semaphore_signal(barrier, inc=1, device_id=at(x, zpeer(i), y), device_id_type=MESH)
        return c

    def greet_xy(i, c):
        q = xypeer(i)
        pl.semaphore_signal(barrier, inc=1, device_id=at(q // 4, z, q % 4), device_id_type=MESH)
        return c

    lax.fori_loop(1, NZ, greet_z, 0)
    lax.fori_loop(1, NXY, greet_xy, 0)
    pl.semaphore_signal(barrier, inc=1, device_id=partner, device_id_type=MESH)

    loads = [
        pltpu.make_async_copy(a, b, in_s.at[i])
        for i, (a, b) in enumerate(
            [
                (wig_in, wig), (feat, fall.at[z, pl.ds(0, 784)]), (cot, cpad.at[pl.ds(0, 784)]),
                (w0_in, w0), (w1_in, w1), (w2_in, w2),
            ]
        )
    ]
    for load in loads:
        load.start()

    trow = jnp.broadcast_to(tgt[...], (EDGES, EDGES)).astype(F32)
    tcol = jnp.transpose(trow)
    earlier = (tcol == trow) & (iota((EDGES, EDGES), 0) < iota((EDGES, EDGES), 1))
    rank = jnp.sum(earlier.astype(F32), axis=0, keepdims=True).astype(jnp.int32)
    t = tgt[...]
    pos = ((t >> 2) & 7) * 32 + ((t >> 5) * 4 + (t & 3)) * 2 + rank
    line = iota((16, EDGES), 0)
    code = jnp.zeros((16, EDGES), jnp.int32)
    for i, row in enumerate([pos, ang[...], src[...] + 1, dat[...] + 1]):
        code = jnp.where(line == i, jnp.broadcast_to(row, (16, EDGES)), code)
    crow[z] = code.astype(F32).astype(BF)

    def expand(q):
        c = crow[q].astype(F32)
        hot = (iota((32, EDGES), 0) + 32 * z).astype(F32) == jnp.broadcast_to(c[0:1], (32, EDGES))
        wide = jnp.concatenate([jnp.broadcast_to(c[i : i + 1], (EDGES, EDGES)) for i in (1, 2, 3)], axis=0)
        got = lax.dot_general(
            hot.astype(BF), wide.astype(BF), (((1,), (1,)), ((), ())), preferred_element_type=F32
        )
        for i in range(3):
            codes[q, i] = got[:, 128 * i : 128 * i + 128].astype(BF)

    for q in range(NZ):
        fall[q, 784:832] = jnp.zeros((48, 128), BF)

    def exchange(step, piece, i):
        q = xypeer(i)
        part = pl.ds(0, SPLIT) if piece == 0 else pl.ds(SPLIT, WIRE - SPLIT)
        return remote(
            sendb.at[step, part, q], recvb.at[part, step, xy], ex_s.at[step], ex_r.at[step], at(q // 4, z, q % 4)
        )

    def own_copy(step):
        return pltpu.make_async_copy(sendb.at[step, :, xy], recvb.at[:, step, xy], loc_s.at[step])

    def rotate(step, piece, zz):
        rows = pl.ds(pl.multiple_of(zz * 32, 32), 32)
        for degree in range(5) if piece == 0 else range(5, LMAX + 1):
            w = width(degree)
            ks = [k for k in range(KEPT) if DEGREE[k] == degree]
            lhs = jnp.concatenate([left[k, rows, 0:w] for k in ks], axis=0)
            lo = ATOMS * degree * degree
            if piece == 0:
                w = min(w, 400 - lo)
                lhs = lhs[:, 0:w]
            got = dot(lhs, fall[zz, lo : lo + w]).astype(BF)
            for i, k in enumerate(ks):
                sendb[step, PLACE[k]] = got[32 * i : 32 * i + 32].reshape(NXY, 2, 128)
        if piece == 0:
            sendb[step, CODE] = codes[zz, 0].reshape(NXY, 2, 128)
            sendb[step, CODE + 1] = codes[zz, 2].reshape(NXY, 2, 128)

    def send_block(step, piece):
        def go(i, c):
            exchange(step, piece, i).start()
            return c

        lax.fori_loop(1, NXY, go, 0)
        if piece:
            own_copy(step).start()

    def whole(step):
        part = recvb.at[:, step, pl.ds(0, NXY - 1)]
        return remote(part, part, ex_s.at[step], ex_r.at[step], at(x, z, y))

    def receive_block(step):
        whole(step).wait_recv()
        own_copy(step).wait()

    loads[1].wait()
    pl.semaphore_wait(barrier, 23)

    def code_copy(i):
        return remote(crow.at[z], crow.at[z], code_s.at[i], code_r.at[i], at(x, zpeer(i), y))

    def code_in(i):
        q = lax.rem(z - i + NZ, NZ)
        return remote(crow.at[q], crow.at[q], code_s.at[i], code_r.at[i], at(x, zpeer(i), y))

    def send_code(i, c):
        code_copy(i).start()
        return c

    def wait_code(i, c):
        code_in(i).wait_recv()
        return c

    def sent_code(i, c):
        code_copy(i).wait_send()
        return c

    lax.fori_loop(1, NZ, send_code, 0)

    def ring(hop, piece, block, direction):
        dev = at(x, lax.rem(z + direction + NZ, NZ), y)
        part = fall.at[block, pl.ds(400 * piece, 400 - 16 * piece)]
        return remote(part, part, ring_s.at[hop, piece], ring_r.at[hop, piece], dev)

    def behind(n):
        return lax.rem(z - sign * n + 2 * NZ, NZ)

    def ahead(n):
        return lax.rem(z + sign * n + 2 * NZ, NZ)

    for piece in range(2):
        ring(0, piece, z, sign).start()
    loads[0].wait()
    build_table(wig, wk, table)
    for piece in range(2):
        ring(4, piece, z, -sign).start()
    expand(z)
    mine = pl.ds(pl.multiple_of(z * 32, 32), 32)
    build_rotation(codes[z, 0].astype(F32), codes[z, 1].astype(F32), table, left, [mine])
    for piece in range(2):
        rotate(0, piece, z)
        send_block(0, piece)
    cpad[784:832] = jnp.zeros((48, 128), BF)

    def prepare(blocks):
        for q in blocks:
            expand(q)
        rows = [pl.ds(pl.multiple_of(q * 32, 32), 32) for q in blocks]
        build_rotation(
            jnp.concatenate([codes[q, 0] for q in blocks], axis=0).astype(F32),
            jnp.concatenate([codes[q, 1] for q in blocks], axis=0).astype(F32),
            table, left, rows,
        )

    def half(h):
        rows = pl.ds(128 * h, 128)

        def rot(k):
            return recvb[k, 4 * h : 4 * h + 4].reshape(128, 128)

        build_rotation(rot(CODE).astype(F32), rot(CODE + 1).astype(F32), table, leftd, [rows])
        for k in range(KEPT):
            w = width(DEGREE[k])
            lo = ATOMS * DEGREE[k] * DEGREE[k]
            pull[k, rows] = dot(leftd[k, rows, 0:w], cpad[lo : lo + w]).astype(BF)
            xt[k, :, rows] = jnp.transpose(rot(PLACE[k]).astype(F32)).astype(BF)

    def pass_on(n, piece, back):
        if back:
            ring(n - 1, piece, behind(n), sign).wait_recv()
            if n < 4:
                ring(n, piece, behind(n), sign).start()
        elif n < 4:
            ring(3 + n, piece, ahead(n), -sign).wait_recv()
            if n < 3:
                ring(4 + n, piece, ahead(n), -sign).start()

    code_in(1).wait_recv()
    code_in(NZ - 1).wait_recv()
    prepare([behind(1), ahead(1)])
    for n in range(1, 5):
        for back in (True, False):
            if n == 4 and not back:
                break
            step = 2 * n - 1 if back else 2 * n
            for piece in range(2):
                pass_on(n, piece, back)
                if n == 2 and back and piece == 0:
                    lax.fori_loop(2, NZ - 1, wait_code, 0)
                    prepare([behind(2), ahead(2), behind(3), ahead(3), behind(4)])
                rotate(step, piece, behind(n) if back else ahead(n))
                send_block(step, piece)
    loads[2].wait()
    for early in range(4):
        receive_block(early)
    half(0)
    for late in range(4, NZ):
        receive_block(late)
    half(1)

    def spread(res, base, length, lo, width_):
        for jb in range(lo, lo + width_):
            flat[pl.ds(base + jb, 128 * length, stride=length), :] = res[:, 128 * (jb - lo) : 128 * (jb - lo) + 128]

    def grads(m):
        if m == 0:
            zt = jnp.concatenate([xt[k] for k in range(7)], axis=0)
            for lo in range(0, 7, 2):
                n = min(2, 7 - lo)
                rhs = jnp.concatenate([pull[lo + i] for i in range(n)], axis=1)
                spread(dot(zt, rhs), 0, 7, lo, n)
            return
        base = 128 * (49 if m == 1 else 49 + 72)
        plus, length = GROUPS[2 * m - 1]
        minus = GROUPS[2 * m][0]
        pqt = jnp.concatenate(
            [jnp.concatenate([xt[plus + i], xt[minus + i]], axis=1) for i in range(length)], axis=0
        )
        for lo in range(0, length, 2):
            n = min(2, length - lo)
            gg = jnp.concatenate([pull[plus + lo + i] for i in range(n)], axis=1)
            hh = jnp.concatenate([pull[minus + lo + i] for i in range(n)], axis=1)
            spread(dot(pqt, jnp.concatenate([gg, hh], axis=0)), base, length, lo, n)
            spread(dot(pqt, jnp.concatenate([hh, -gg], axis=0)), base + 128 * length * length, length, lo, n)

    def pack(s, c):
        pk[s] = flat[pl.ds(SHARD * s + HALF * (1 - dp), HALF), :].astype(BF)
        return c

    def merge(s, c):
        sx = s // 32
        cz = (s // 4) % 8
        sy = s % 4
        both = (flat[pl.ds(SHARD * s + HALF * dp, HALF), :] + r0[s].astype(F32)).astype(BF)
        s0[0, sx, sy, cz] = both[0:RING]
        s0[1, sy, sx, cz] = both[RING : 2 * RING]
        sz[cz, sx * 4 + sy] = both[2 * RING : HALF]
        return c

    flat[ROWS : ROWS + 24] = jnp.zeros((24, 128), F32)
    runs = [(0, 36), (36, 90), (90, 128)]
    swaps = []
    for m, (lo, hi) in enumerate(runs):
        grads(m)
        lax.fori_loop(lo, hi, pack, 0)
        part = pl.ds(lo, hi - lo)
        swaps.append(remote(pk.at[part], r0.at[part], dp_s.at[m], dp_r.at[m], partner))
        swaps[m].start()
    for m, (lo, hi) in enumerate(runs):
        swaps[m].wait()
        lax.fori_loop(lo, hi, merge, 0)

    def mixed(k):
        return recvb[k].reshape(SLOTS, 128)

    def cat(ks):
        return jnp.concatenate([mixed(PLACE[k]) for k in ks], axis=1)

    message = {}

    def mix(m):
        if m == 0:
            zero = dot(cat(range(7)), w0[...]).astype(BF)
            for i in range(7):
                message[i] = zero[:, 128 * i : 128 * i + 128]
            return
        w = w1 if m == 1 else w2
        plus, length = GROUPS[2 * m - 1]
        minus = GROUPS[2 * m][0]
        p, q = cat(range(plus, plus + length)), cat(range(minus, minus + length))
        up = (dot(p, w[0]) - dot(q, w[1])).astype(BF)
        um = (dot(p, w[1]) + dot(q, w[0])).astype(BF)
        for i in range(length):
            message[plus + i] = up[:, 128 * i : 128 * i + 128]
            message[minus + i] = um[:, 128 * i : 128 * i + 128]

    def gather_atoms():
        for degree in range(LMAX + 1):
            w = width(degree)
            ks = [k for k in range(KEPT) if DEGREE[k] == degree]
            lhs = jnp.concatenate([leftd[k, :, 0:w] for k in ks], axis=0)
            rhs = jnp.concatenate([message[k] for k in ks], axis=0)
            got = lax.dot_general(lhs, rhs, (((0,), (0,)), ((), ())), preferred_element_type=F32)
            size = 2 * degree + 1
            agg[degree * degree : (degree + 1) * (degree + 1)] = (
                got[0 : ATOMS * size].astype(BF).reshape(size, ATOMS, 128)
            )

    def along_x(d):
        return at(lax.rem(x + d + NX, NX), z, y)

    def along_y(d):
        return at(x, z, lax.rem(y + d + NY, NY))

    def mod4(v):
        return lax.rem(v + 4, 4)

    parts = [(0, x, along_x, y, along_y), (1, y, along_y, x, along_x)]
    one, two, three, subs = [], [], [], []
    for i, p, move, q, _ in parts:
        order = [mod4(q + 2 * sign), mod4(q - sign), mod4(q + sign), q]
        subs.append(order)
        one.append(
            [remote(s0.at[i, mod4(p + 2 * sign), j], ra.at[i, j], st_s.at[i, 0, n], st_r.at[i, 0, n], move(sign))
             for n, j in enumerate(order)]
        )
        two.append(
            [remote(s0.at[i, mod4(p - sign), j], rb.at[i, j], st_s.at[i, 1, n], st_r.at[i, 1, n], move(-sign))
             for n, j in enumerate(order)]
        )
        three.append(
            [remote(ta.at[i, j], rc.at[i, j], st_s.at[i, 2, n], st_r.at[i, 2, n], move(sign))
             for n, j in enumerate(order)]
        )
    def mod8(v):
        return lax.rem(v + 8, 8)

    def up(h, j):
        src = sz.at[mod8(z + 4 * sign), pl.ds(8 * j, 8)] if h == 0 else va.at[h - 1, j]
        return remote(src, ua.at[h, j], ua_s.at[h, j], ua_r.at[h, j], at(x, mod8(z + sign), y))

    def down(h, j):
        src = sz.at[mod8(z - 3 * sign), pl.ds(8 * j, 8)] if h == 0 else vb.at[h - 1, j]
        return remote(src, ub.at[h, j], ub_s.at[h, j], ub_r.at[h, j], at(x, mod8(z - sign), y))

    def pass_sum(h, j):
        part = pl.ds(8 * j, 8)
        up(h, j).wait_recv()
        va[h, j] = (ua[h, j].astype(F32) + sz[mod8(z + (3 - h) * sign), part].astype(F32)).astype(BF)
        up(h + 1, j).start()
        if h < 2:
            down(h, j).wait_recv()
            vb[h, j] = (ub[h, j].astype(F32) + sz[mod8(z - (2 - h) * sign), part].astype(F32)).astype(BF)
            down(h + 1, j).start()

    def end_sum(j):
        part = pl.ds(8 * j, 8)
        up(3, j).wait_recv()
        down(2, j).wait_recv()
        sz1[part] = (sz[z, part].astype(F32) + ua[3, j].astype(F32) + ub[2, j].astype(F32)).astype(BF)

    def relay(n):
        for i, p, *_ in parts:
            j = subs[i][n]
            one[i][n].wait_recv()
            ta[i, j] = (ra[i, j].astype(F32) + s0[i, mod4(p + sign), j].astype(F32)).astype(BF)
            three[i][n].start()

    four, five, six = [], [], []
    for i, p, _, q, move in parts:
        order = subs[i]
        four.append(remote(s1.at[i, order[0]], ra1.at[i], su_s.at[i, 0], su_r.at[i, 0], move(sign)))
        five.append(remote(s1.at[i, order[1]], rb1.at[i], su_s.at[i, 1], su_r.at[i, 1], move(-sign)))
        six.append(remote(ta1.at[i], rc1.at[i], su_s.at[i, 2], su_r.at[i, 2], move(sign)))

    def close(n):
        for i, p, *_ in parts:
            j = subs[i][n]
            two[i][n].wait_recv()
            three[i][n].wait_recv()
            s1[i, j] = (s0[i, p, j].astype(F32) + rb[i, j].astype(F32) + rc[i, j].astype(F32)).astype(BF)
            if n == 0:
                four[i].start()
            if n == 1:
                five[i].start()

    for j in range(2):
        up(0, j).start()
        down(0, j).start()
    for n in range(4):
        for i in range(2):
            one[i][n].start()
            two[i][n].start()
    for load in loads[3:]:
        load.wait()
    mix(1)
    mix(2)
    pass_sum(0, 0)
    relay(0)
    pass_sum(0, 1)
    relay(1)
    mix(0)
    pass_sum(1, 0)
    relay(2)
    pass_sum(1, 1)
    relay(3)
    pass_sum(2, 0)
    close(0)
    pass_sum(2, 1)
    for n in range(1, 4):
        close(n)
    for i in range(2):
        four[i].wait_recv()
        ta1[i] = (ra1[i].astype(F32) + s1[i, subs[i][2]].astype(F32)).astype(BF)
        six[i].start()
    for j in range(2):
        end_sum(j)

    def across(i):
        q = xypeer(i)
        return remote(sz1.at[q], r4.at[i], w_s.at[i], w_r.at[i], at(q // 4, z, q % 4))

    def across_go(i, c):
        across(i).start()
        return c

    lax.fori_loop(1, NXY, across_go, 0)
    gather_atoms()
    store_agg = pltpu.make_async_copy(agg, agg_out, out_s.at[0])
    store_agg.start()
    for i in range(2):
        five[i].wait_recv()
        six[i].wait_recv()
        s2[i] = (s1[i, subs[i][3]].astype(F32) + rb1[i].astype(F32) + rc1[i].astype(F32)).astype(BF)

    def zcopy(a, i):
        q = zpeer(i)
        return remote(s2.at[a, q], r3.at[a, i], z_s.at[a, i], z_r.at[a, i], at(x, q, y))

    for a in range(2):

        def zgo(i, c):
            zcopy(a, i).start()
            return c

        lax.fori_loop(1, NZ, zgo, 0)
    total = sz1[xy].astype(F32)
    for i in range(1, NXY):
        across(i).wait()
        total = total + r4[i].astype(F32)
    fin[2 * RING : HALF] = total
    for a in range(2):
        total = s2[a, z].astype(F32)
        for i in range(1, NZ):
            zcopy(a, i).wait()
            total = total + r3[a, i].astype(F32)
        fin[RING * a : RING * a + RING] = total
    mine = wgrad.at[pl.ds(pl.multiple_of(HALF * dp, 8), HALF)]
    last = remote(fin, mine, f_s, f_r, partner)
    last.start()
    store = pltpu.make_async_copy(fin, mine, out_s.at[1])
    store.start()
    for j in range(2):
        for h in range(4):
            up(h, j).wait_send()
        for h in range(3):
            down(h, j).wait_send()
    for n in range(4):
        for i in range(2):
            one[i][n].wait_send()
            two[i][n].wait_send()
            three[i][n].wait_send()
    for i in range(2):
        four[i].wait_send()
        five[i].wait_send()
        six[i].wait_send()
    for piece in range(2):
        for n in range(4):
            ring(n, piece, z, sign).wait_send()
        for n in range(3):
            ring(4 + n, piece, z, -sign).wait_send()
    for step in range(NZ):
        whole(step).wait_send()
    lax.fori_loop(1, NZ, sent_code, 0)
    store_agg.wait()
    store.wait()
    last.wait()


def finish(agg_in, wgrad_in, agg, wgrad):
    agg[...] = agg_in[...]
    wgrad[...] = wgrad_in[0:SHARD]


def shards(features, cotangent, wigner, src_atom, dst_part, dst_atom, angle, w_zero, w_one, w_two):
    dma = pltpu.SemaphoreType.DMA
    scratch = [
        pltpu.VMEM((49, ATOMS, 128), BF),
        pltpu.VMEM((49, KEPT, 256), BF),
        pltpu.VMEM(w_zero.shape, BF),
        pltpu.VMEM(w_one.shape, BF),
        pltpu.VMEM(w_two.shape, BF),
        pltpu.VMEM((KEPT, SLOTS, 256), BF),
        pltpu.VMEM((KEPT, 64, 256), BF),
        pltpu.VMEM((KEPT, SLOTS, 256), BF),
        pltpu.VMEM((KEPT, SLOTS, 256), BF),
        pltpu.VMEM((NZ, 16, 128), BF),
        pltpu.VMEM((NZ, 3, 32, 128), BF),
        pltpu.VMEM((NZ, 832, 128), BF),
        pltpu.VMEM((832, 128), BF),
        pltpu.VMEM((NZ, WIRE, NXY, 2, 128), BF),
        pltpu.VMEM((WIRE, NZ, NXY, 2, 128), BF),
        pltpu.VMEM((KEPT, SLOTS, 128), BF),
        pltpu.VMEM((KEPT, 128, SLOTS), BF),
        pltpu.VMEM((ROWS + 24, 128), F32),
        pltpu.VMEM((128, HALF, 128), BF),
        pltpu.VMEM((128, HALF, 128), BF),
        pltpu.VMEM((2, 4, 4, NZ, RING, 128), BF),
    ]
    scratch += [pltpu.VMEM((2, 4, NZ, RING, 128), BF) for _ in range(4)]
    scratch += [pltpu.VMEM((2, 4, NZ, RING, 128), BF)]
    scratch += [pltpu.VMEM((2, NZ, RING, 128), BF) for _ in range(4)]
    scratch += [pltpu.VMEM((2, NZ, RING, 128), BF)]
    scratch += [
        pltpu.VMEM((2, NZ, RING, 128), BF),
        pltpu.VMEM((HALF, 128), F32),
        pltpu.VMEM((NZ, NXY, REST, 128), BF),
        pltpu.VMEM((4, 2, 8, REST, 128), BF),
        pltpu.VMEM((3, 2, 8, REST, 128), BF),
        pltpu.VMEM((3, 2, 8, REST, 128), BF),
        pltpu.VMEM((2, 2, 8, REST, 128), BF),
        pltpu.VMEM((NXY, REST, 128), BF),
        pltpu.VMEM((NXY, REST, 128), BF),
        dma((NZ,)), dma((NZ,)),
        dma((7, 2)), dma((7, 2)),
        dma((NZ,)), dma((NZ,)), dma((NZ,)),
        dma((3,)), dma((3,)),
        dma((2, 3, 4)), dma((2, 3, 4)),
        dma((2, 3)), dma((2, 3)),
        dma((2, NZ)), dma((2, NZ)),
        dma, dma,
        dma((6,)), dma((2,)),
        dma((4, 2)), dma((4, 2)), dma((3, 2)), dma((3, 2)), dma((NXY,)), dma((NXY,)),
    ]
    vmem = pl.BlockSpec(memory_space=pltpu.VMEM)
    agg, wgrad = pl.pallas_call(
        kernel,
        out_shape=(
            jax.ShapeDtypeStruct((49, ATOMS, 128), BF),
            jax.ShapeDtypeStruct((2 * HALF, 128), F32),
        ),
        in_specs=[vmem] * 4 + [pl.BlockSpec(memory_space=pl.ANY)] * 6,
        out_specs=(pl.BlockSpec(memory_space=pl.ANY),) * 2,
        scratch_shapes=scratch,
        compiler_params=pltpu.CompilerParams(
            collective_id=0, has_side_effects=True, vmem_limit_bytes=67000000
        ),
    )(
        dst_part.reshape(1, EDGES),
        src_atom.reshape(1, EDGES),
        dst_atom.reshape(1, EDGES),
        angle.reshape(1, EDGES),
        jnp.transpose(wigner, (2, 1, 0)),
        jnp.transpose(features, (1, 0, 2)).reshape(784, 128),
        jnp.transpose(cotangent, (1, 0, 2)).reshape(784, 128),
        w_zero, w_one, w_two,
    )
    agg, wgrad = pl.pallas_call(
        finish,
        out_shape=(
            jax.ShapeDtypeStruct((49, ATOMS, 128), BF),
            jax.ShapeDtypeStruct((SHARD, 128), F32),
        ),
        in_specs=[vmem] * 2,
        out_specs=(vmem, vmem),
    )(agg, wgrad)
    return jnp.transpose(agg, (1, 0, 2)), wgrad.reshape(SHARD * 128)


def solution(mesh):
    both = ("dp", "graph")
    placed = (
        P(both, None, None), P(both, None, None), P(), P(both), P(both, None), P(both), P(both), P(), P(), P(),
    )
    return jax.shard_map(
        shards,
        mesh=mesh,
        in_specs=placed,
        out_specs=(P(both, None, None), P("graph")),
        check_vma=False,
    )
```

```python
import functools

import jax
import jax.numpy as jnp
from jax import lax
from jax.experimental import pallas as pl
from jax.experimental.pallas import tpu as pltpu
from jax.sharding import PartitionSpec as P

LMAX = 6
MMAX = 2
NX, NZ, NY = 4, 8, 4
NXY = NX * NY
EDGES = 128
ATOMS = 16
SLOTS = 256
ROWS = 21888
SHARD = 171
HALF = 88
RING = 32
REST = 24
MESH = pl.DeviceIdType.MESH
BF = jnp.bfloat16
F32 = jnp.float32


def kept_degrees():
    out = list(range(LMAX + 1))
    for m in range(1, MMAX + 1):
        for _ in range(2):
            out.extend(range(m, LMAX + 1))
    return out


DEGREE = kept_degrees()
KEPT = len(DEGREE)
WIRE = KEPT + 1
SPLIT = 20
CODE = SPLIT - 1
BY_DEGREE = sorted(range(KEPT), key=lambda k: (DEGREE[k], k))
PLACE = {k: i if i < CODE else i + 1 for i, k in enumerate(BY_DEGREE)}
GROUPS = [(0, 7), (7, 6), (13, 6), (19, 5), (24, 5)]


def width(degree):
    return 128 if degree <= 3 else 256


def dot(a, b):
    return jnp.dot(a, b, preferred_element_type=F32)


def iota(shape, dim):
    return lax.broadcasted_iota(jnp.int32, shape, dim)


def remote(src, dst, send, recv, device):
    return pltpu.make_async_remote_copy(
        src_ref=src, dst_ref=dst, send_sem=send, recv_sem=recv, device_id=device, device_id_type=MESH
    )


def build_table(wig, wk, table):
    wk[...] = jnp.zeros_like(wk)
    wk[:, 0:49, :] = jnp.swapaxes(wig[...].astype(F32), 0, 1).astype(BF)
    for degree in range(LMAX + 1):
        w = width(degree)
        j = iota((w, 64), 1)
        n = iota((w, 64), 0)
        spread = ((j == degree * degree + n // ATOMS) & (n < ATOMS * (2 * degree + 1))).astype(BF)
        for k in [k for k in range(KEPT) if DEGREE[k] == degree]:
            table[k, 0:w] = dot(spread, wk[k]).astype(BF)


def build_rotation(angle, atom, table, left, rows):
    size = angle.shape[0]
    lane = iota((size, 128), 1)
    near = (angle == lane.astype(F32)).astype(BF)
    far = (angle == (lane + 128).astype(F32)).astype(BF)
    pick = jnp.concatenate([near, far], axis=1)
    mask = (atom == (lane % ATOMS + 1).astype(F32)).astype(F32)
    wide = jnp.concatenate([mask, mask], axis=1)
    for k in range(KEPT):
        w = width(DEGREE[k])
        gate = mask if w == 128 else wide
        got = lax.dot_general(pick, table[k, 0:w], (((1,), (1,)), ((), ())), preferred_element_type=F32)
        got = (got * gate).astype(BF)
        step = size // len(rows)
        for i, part in enumerate(rows):
            left[k, part, 0:w] = got[step * i : step * i + step]


def kernel(
    tgt, src, dat, ang, wig_in, feat, cot, w0_in, w1_in, w2_in,
    agg_out, wgrad,
    agg, wig, w0, w1, w2, table, wk, left, leftd, crow, codes, fall, cpad, sendb, recvb, pull, xt, flat,
    pk, r0, s0, ra, ta, rb, rc, s1, ra1, ta1, rb1, rc1, s2, r3, fin,
    sz, ua, va, ub, vb, sz1, r4,
    code_s, code_r, ring_s, ring_r, ex_s, ex_r, loc_s, dp_s, dp_r, st_s, st_r, su_s, su_r, z_s, z_r, f_s, f_r, in_s, out_s,
    ua_s, ua_r, ub_s, ub_r, w_s, w_r,
):
    dp = lax.axis_index("dp")
    g = lax.axis_index("graph")
    x = g // 32
    z = (g // 4) % 8
    y = g % 4
    xy = x * 4 + y
    sign = 1 - 2 * dp

    def at(px, pz, py):
        return (dp, px * 32 + pz * 4 + py)

    partner = (1 - dp, g)

    def zpeer(i):
        return lax.rem(z + i, NZ)

    def xypeer(i):
        return lax.rem(xy + i, NXY)

    barrier = pltpu.get_barrier_semaphore()

    def greet_z(i, c):
        pl.semaphore_signal(barrier, inc=1, device_id=at(x, zpeer(i), y), device_id_type=MESH)
        return c

    def greet_xy(i, c):
        q = xypeer(i)
        pl.semaphore_signal(barrier, inc=1, device_id=at(q // 4, z, q % 4), device_id_type=MESH)
        return c

    lax.fori_loop(1, NZ, greet_z, 0)
    lax.fori_loop(1, NXY, greet_xy, 0)
    pl.semaphore_signal(barrier, inc=1, device_id=partner, device_id_type=MESH)

    loads = [
        pltpu.make_async_copy(a, b, in_s.at[i])
        for i, (a, b) in enumerate(
            [
                (wig_in, wig), (feat, fall.at[z, pl.ds(0, 784)]), (cot, cpad.at[pl.ds(0, 784)]),
                (w0_in, w0), (w1_in, w1), (w2_in, w2),
            ]
        )
    ]
    for load in loads:
        load.start()

    trow = jnp.broadcast_to(tgt[...], (EDGES, EDGES)).astype(F32)
    tcol = jnp.transpose(trow)
    earlier = (tcol == trow) & (iota((EDGES, EDGES), 0) < iota((EDGES, EDGES), 1))
    rank = jnp.sum(earlier.astype(F32), axis=0, keepdims=True).astype(jnp.int32)
    t = tgt[...]
    pos = ((t >> 2) & 7) * 32 + ((t >> 5) * 4 + (t & 3)) * 2 + rank
    line = iota((16, EDGES), 0)
    code = jnp.zeros((16, EDGES), jnp.int32)
    for i, row in enumerate([pos, ang[...], src[...] + 1, dat[...] + 1]):
        code = jnp.where(line == i, jnp.broadcast_to(row, (16, EDGES)), code)
    crow[z] = code.astype(F32).astype(BF)

    def expand(q):
        c = crow[q].astype(F32)
        hot = (iota((32, EDGES), 0) + 32 * z).astype(F32) == jnp.broadcast_to(c[0:1], (32, EDGES))
        wide = jnp.concatenate([jnp.broadcast_to(c[i : i + 1], (EDGES, EDGES)) for i in (1, 2, 3)], axis=0)
        got = lax.dot_general(
            hot.astype(BF), wide.astype(BF), (((1,), (1,)), ((), ())), preferred_element_type=F32
        )
        codes[q, 0] = got[:, 0:128].astype(BF)
        codes[q, 1] = got[:, 128:256].astype(BF)
        codes[q, 2] = jnp.where(iota((32, 128), 1) < 64, got[:, 0:128], got[:, 256:384]).astype(BF)

    for q in range(NZ):
        fall[q, 784:832] = jnp.zeros((48, 128), BF)

    def exchange(step, piece, i):
        q = xypeer(i)
        part = pl.ds(0, SPLIT) if piece == 0 else pl.ds(SPLIT, WIRE - SPLIT)
        return remote(
            sendb.at[step, part, q], recvb.at[part, step, xy], ex_s, ex_r.at[step // 4], at(q // 4, z, q % 4)
        )

    def own_copy(step):
        return pltpu.make_async_copy(sendb.at[step, :, xy], recvb.at[:, step, xy], loc_s.at[step // 4])

    def rotate(step, piece, zz):
        rows = pl.ds(pl.multiple_of(zz * 32, 32), 32)
        for degree in range(5) if piece == 0 else range(5, LMAX + 1):
            w = width(degree)
            ks = [k for k in range(KEPT) if DEGREE[k] == degree]
            lhs = jnp.concatenate([left[k, rows, 0:w] for k in ks], axis=0)
            lo = ATOMS * degree * degree
            if piece == 0:
                w = min(w, 400 - lo)
                lhs = lhs[:, 0:w]
            got = dot(lhs, fall[zz, lo : lo + w]).astype(BF)
            for i, k in enumerate(ks):
                sendb[step, PLACE[k]] = got[32 * i : 32 * i + 32].reshape(NXY, 2, 128)
        if piece == 0:
            sendb[step, CODE] = codes[zz, 2].reshape(NXY, 2, 128)

    def send_block(step, piece):
        def go(i, c):
            exchange(step, piece, i).start()
            return c

        lax.fori_loop(1, NXY, go, 0)
        if piece:
            own_copy(step).start()

    def receive_half(h):
        part = recvb.at[:, pl.ds(4 * h, 4), pl.ds(0, NXY - 1)]
        remote(part, part, ex_s, ex_r.at[h], partner).wait_recv()
        part = recvb.at[:, pl.ds(4 * h, 4), 0]
        pltpu.make_async_copy(part, part, loc_s.at[h]).wait()

    loads[1].wait()
    pl.semaphore_wait(barrier, 23)

    def code_copy(i):
        lane = 0 if i == 1 else 1 if i == NZ - 1 else 2
        return remote(crow.at[z], crow.at[z], code_s, code_r.at[lane], at(x, zpeer(i), y))

    def code_all(count, lane):
        part = crow.at[pl.ds(0, count)]
        return remote(part, part, code_s, code_r.at[lane], partner)

    for i in range(1, NZ):
        code_copy(i).start()

    def ring(hop, piece, block, direction):
        dev = at(x, lax.rem(z + direction + NZ, NZ), y)
        part = fall.at[block, pl.ds(400 * piece, 400 - 16 * piece)]
        return remote(part, part, ring_s, ring_r.at[hop, piece], dev)

    def behind(n):
        return lax.rem(z - sign * n + 2 * NZ, NZ)

    def ahead(n):
        return lax.rem(z + sign * n + 2 * NZ, NZ)

    for piece in range(2):
        ring(0, piece, z, sign).start()
    loads[0].wait()
    build_table(wig, wk, table)
    for piece in range(2):
        ring(4, piece, z, -sign).start()
    expand(z)
    mine = pl.ds(pl.multiple_of(z * 32, 32), 32)
    build_rotation(codes[z, 0].astype(F32), codes[z, 1].astype(F32), table, left, [mine])
    for piece in range(2):
        rotate(0, piece, z)
        send_block(0, piece)
    cpad[784:832] = jnp.zeros((48, 128), BF)

    def prepare(blocks):
        for q in blocks:
            expand(q)
        rows = [pl.ds(pl.multiple_of(q * 32, 32), 32) for q in blocks]
        build_rotation(
            jnp.concatenate([codes[q, 0] for q in blocks], axis=0).astype(F32),
            jnp.concatenate([codes[q, 1] for q in blocks], axis=0).astype(F32),
            table, left, rows,
        )

    def half(h):
        rows = pl.ds(128 * h, 128)

        def rot(k):
            return recvb[k, 4 * h : 4 * h + 4].reshape(128, 128)

        r, c = iota((128, 256), 0), iota((128, 256), 1)
        parted = dot(rot(CODE), (r == jnp.where(c < 128, 0, 64)).astype(BF))
        build_rotation(parted[:, 0:128], parted[:, 128:256], table, leftd, [rows])
        for k in range(KEPT):
            w = width(DEGREE[k])
            lo = ATOMS * DEGREE[k] * DEGREE[k]
            pull[k, rows] = dot(leftd[k, rows, 0:w], cpad[lo : lo + w]).astype(BF)
            xt[k, :, rows] = jnp.transpose(rot(PLACE[k]).astype(F32)).astype(BF)

    def pass_on(n, piece, back):
        if back:
            ring(n - 1, piece, behind(n), sign).wait_recv()
            if n < 4:
                ring(n, piece, behind(n), sign).start()
        elif n < 4:
            ring(3 + n, piece, ahead(n), -sign).wait_recv()
            if n < 3:
                ring(4 + n, piece, ahead(n), -sign).start()

    code_all(1, 0).wait_recv()
    code_all(1, 1).wait_recv()
    prepare([behind(1), ahead(1)])
    for n in range(1, 5):
        for back in (True, False):
            if n == 4 and not back:
                break
            step = 2 * n - 1 if back else 2 * n
            for piece in range(2):
                pass_on(n, piece, back)
                if n == 2 and back and piece == 0:
                    code_all(5, 2).wait_recv()
                    prepare([behind(2), ahead(2), behind(3), ahead(3), behind(4)])
                rotate(step, piece, behind(n) if back else ahead(n))
                send_block(step, piece)
    loads[2].wait()
    receive_half(0)
    half(0)
    receive_half(1)
    half(1)

    def spread(res, base, length, lo, width_):
        for jb in range(lo, lo + width_):
            flat[pl.ds(base + jb, 128 * length, stride=length), :] = res[:, 128 * (jb - lo) : 128 * (jb - lo) + 128]

    def grads(m):
        if m == 0:
            zt = jnp.concatenate([xt[k] for k in range(7)], axis=0)
            for lo in range(0, 7, 2):
                n = min(2, 7 - lo)
                rhs = jnp.concatenate([pull[lo + i] for i in range(n)], axis=1)
                spread(dot(zt, rhs), 0, 7, lo, n)
            return
        base = 128 * (49 if m == 1 else 49 + 72)
        plus, length = GROUPS[2 * m - 1]
        minus = GROUPS[2 * m][0]
        pqt = jnp.concatenate(
            [jnp.concatenate([xt[plus + i], xt[minus + i]], axis=1) for i in range(length)], axis=0
        )
        for lo in range(0, length, 2):
            n = min(2, length - lo)
            gg = jnp.concatenate([pull[plus + lo + i] for i in range(n)], axis=1)
            hh = jnp.concatenate([pull[minus + lo + i] for i in range(n)], axis=1)
            spread(dot(pqt, jnp.concatenate([gg, hh], axis=0)), base, length, lo, n)
            spread(dot(pqt, jnp.concatenate([hh, -gg], axis=0)), base + 128 * length * length, length, lo, n)

    def pack(s, c):
        pk[s] = flat[pl.ds(SHARD * s + HALF * (1 - dp), HALF), :].astype(BF)
        return c

    def merge(s, c):
        sx = s // 32
        cz = (s // 4) % 8
        sy = s % 4
        both = (flat[pl.ds(SHARD * s + HALF * dp, HALF), :] + r0[s].astype(F32)).astype(BF)
        s0[0, sx, sy, cz] = both[0:RING]
        s0[1, sy, sx, cz] = both[RING : 2 * RING]
        sz[cz, sx * 4 + sy] = both[2 * RING : HALF]
        return c

    flat[ROWS : ROWS + 24] = jnp.zeros((24, 128), F32)
    runs = [(0, 36), (36, 90), (90, 128)]
    swaps = []
    for m, (lo, hi) in enumerate(runs):
        grads(m)
        lax.fori_loop(lo, hi, pack, 0)
        part = pl.ds(lo, hi - lo)
        swaps.append(remote(pk.at[part], r0.at[part], dp_s, dp_r.at[m], partner))
        swaps[m].start()
    for m, (lo, hi) in enumerate(runs):
        swaps[m].wait_recv()
        lax.fori_loop(lo, hi, merge, 0)

    def mixed(k):
        return recvb[k].reshape(SLOTS, 128)

    def cat(ks):
        return jnp.concatenate([mixed(PLACE[k]) for k in ks], axis=1)

    message = {}

    def mix(m):
        if m == 0:
            zero = dot(cat(range(7)), w0[...]).astype(BF)
            for i in range(7):
                message[i] = zero[:, 128 * i : 128 * i + 128]
            return
        w = w1 if m == 1 else w2
        plus, length = GROUPS[2 * m - 1]
        minus = GROUPS[2 * m][0]
        p, q = cat(range(plus, plus + length)), cat(range(minus, minus + length))
        up = (dot(p, w[0]) - dot(q, w[1])).astype(BF)
        um = (dot(p, w[1]) + dot(q, w[0])).astype(BF)
        for i in range(length):
            message[plus + i] = up[:, 128 * i : 128 * i + 128]
            message[minus + i] = um[:, 128 * i : 128 * i + 128]

    def gather_atoms():
        for degree in range(LMAX + 1):
            w = width(degree)
            ks = [k for k in range(KEPT) if DEGREE[k] == degree]
            lhs = jnp.concatenate([leftd[k, :, 0:w] for k in ks], axis=0)
            rhs = jnp.concatenate([message[k] for k in ks], axis=0)
            got = lax.dot_general(lhs, rhs, (((0,), (0,)), ((), ())), preferred_element_type=F32)
            size = 2 * degree + 1
            agg[degree * degree : (degree + 1) * (degree + 1)] = (
                got[0 : ATOMS * size].astype(BF).reshape(size, ATOMS, 128)
            )

    def along_x(d):
        return at(lax.rem(x + d + NX, NX), z, y)

    def along_y(d):
        return at(x, z, lax.rem(y + d + NY, NY))

    def mod4(v):
        return lax.rem(v + 4, 4)

    parts = [(0, x, along_x, y, along_y), (1, y, along_y, x, along_x)]
    one, two, three, subs = [], [], [], []
    for i, p, move, q, _ in parts:
        order = [mod4(q + 2 * sign), mod4(q - sign), mod4(q + sign), q]
        subs.append(order)
        one.append(
            [remote(s0.at[i, mod4(p + 2 * sign), j], ra.at[i, j], st_s, st_r.at[i, n], move(sign))
             for n, j in enumerate(order)]
        )
        two.append(
            [remote(s0.at[i, mod4(p - sign), j], rb.at[i, j], st_s, st_r.at[i, 8], move(-sign))
             for n, j in enumerate(order)]
        )
        three.append(
            [remote(ta.at[i, j], rc.at[i, j], st_s, st_r.at[i, 4 + n], move(sign))
             for n, j in enumerate(order)]
        )
    def mod8(v):
        return lax.rem(v + 8, 8)

    def up(h, j):
        src = sz.at[mod8(z + 4 * sign), pl.ds(8 * j, 8)] if h == 0 else va.at[h - 1, j]
        return remote(src, ua.at[h, j], ua_s, ua_r.at[h, j], at(x, mod8(z + sign), y))

    def down(h, j):
        src = sz.at[mod8(z - 3 * sign), pl.ds(8 * j, 8)] if h == 0 else vb.at[h - 1, j]
        return remote(src, ub.at[h, j], ub_s, ub_r.at[h, j], at(x, mod8(z - sign), y))

    def pass_sum(h, j):
        part = pl.ds(8 * j, 8)
        up(h, j).wait_recv()
        va[h, j] = (ua[h, j].astype(F32) + sz[mod8(z + (3 - h) * sign), part].astype(F32)).astype(BF)
        up(h + 1, j).start()
        if h < 2:
            down(h, j).wait_recv()
            vb[h, j] = (ub[h, j].astype(F32) + sz[mod8(z - (2 - h) * sign), part].astype(F32)).astype(BF)
            down(h + 1, j).start()

    def end_sum(j):
        part = pl.ds(8 * j, 8)
        up(3, j).wait_recv()
        down(2, j).wait_recv()
        sz1[part] = (sz[z, part].astype(F32) + ua[3, j].astype(F32) + ub[2, j].astype(F32)).astype(BF)

    def relay(n):
        for i, p, *_ in parts:
            j = subs[i][n]
            one[i][n].wait_recv()
            ta[i, j] = (ra[i, j].astype(F32) + s0[i, mod4(p + sign), j].astype(F32)).astype(BF)
            three[i][n].start()

    four, five, six = [], [], []
    for i, p, _, q, move in parts:
        order = subs[i]
        four.append(remote(s1.at[i, order[0]], ra1.at[i], su_s, su_r.at[i, 0], move(sign)))
        five.append(remote(s1.at[i, order[1]], rb1.at[i], su_s, su_r.at[i, 1], move(-sign)))
        six.append(remote(ta1.at[i], rc1.at[i], su_s, su_r.at[i, 2], move(sign)))

    def close(n):
        for i, p, *_ in parts:
            j = subs[i][n]
            if n == 0:
                remote(rb.at[i], rb.at[i], st_s, st_r.at[i, 8], partner).wait_recv()
            three[i][n].wait_recv()
            s1[i, j] = (s0[i, p, j].astype(F32) + rb[i, j].astype(F32) + rc[i, j].astype(F32)).astype(BF)
            if n == 0:
                four[i].start()
            if n == 1:
                five[i].start()

    for j in range(2):
        up(0, j).start()
        down(0, j).start()
    for n in range(4):
        for i in range(2):
            one[i][n].start()
            two[i][n].start()
    for load in loads[3:]:
        load.wait()
    mix(1)
    mix(2)
    pass_sum(0, 0)
    relay(0)
    pass_sum(0, 1)
    relay(1)
    mix(0)
    pass_sum(1, 0)
    relay(2)
    pass_sum(1, 1)
    relay(3)
    pass_sum(2, 0)
    close(0)
    pass_sum(2, 1)
    for n in range(1, 4):
        close(n)
    for i in range(2):
        four[i].wait_recv()
        ta1[i] = (ra1[i].astype(F32) + s1[i, subs[i][2]].astype(F32)).astype(BF)
        six[i].start()
    for j in range(2):
        end_sum(j)

    def across(i):
        q = xypeer(i)
        return remote(sz1.at[q], r4.at[i], w_s, w_r, at(q // 4, z, q % 4))

    def across_go(i, c):
        across(i).start()
        return c

    lax.fori_loop(1, NXY, across_go, 0)
    gather_atoms()
    store_agg = pltpu.make_async_copy(agg, agg_out, out_s.at[0])
    store_agg.start()
    for i in range(2):
        five[i].wait_recv()
        six[i].wait_recv()
        s2[i] = (s1[i, subs[i][3]].astype(F32) + rb1[i].astype(F32) + rc1[i].astype(F32)).astype(BF)

    def zcopy(a, i):
        q = zpeer(i)
        return remote(s2.at[a, q], r3.at[a, i], z_s, z_r.at[a], at(x, q, y))

    for a in range(2):

        def zgo(i, c):
            zcopy(a, i).start()
            return c

        lax.fori_loop(1, NZ, zgo, 0)
    total = sz1[xy].astype(F32)
    part = r4.at[pl.ds(1, NXY - 1)]
    remote(part, part, w_s, w_r, partner).wait()
    for i in range(1, NXY):
        total = total + r4[i].astype(F32)
    fin[2 * RING : HALF] = total
    for a in range(2):
        total = s2[a, z].astype(F32)
        part = r3.at[a, pl.ds(1, NZ - 1)]
        remote(part, part, z_s, z_r.at[a], partner).wait_recv()
        for i in range(1, NZ):
            total = total + r3[a, i].astype(F32)
        fin[RING * a : RING * a + RING] = total
    mine = wgrad.at[pl.ds(pl.multiple_of(HALF * dp, 8), HALF)]
    last = remote(fin, mine, f_s, f_r, partner)
    last.start()
    store = pltpu.make_async_copy(fin, mine, out_s.at[1])
    store.start()
    for part, sem in (
        (ua, ua_s), (ub, ub_s), (s0.at[:, pl.ds(0, 3)], st_s), (s1.at[:, pl.ds(0, 3)], su_s),
        (s2.at[:, pl.ds(0, NZ - 1)], z_s), (pk, dp_s),
    ):
        remote(part, part, sem, f_r, partner).wait_send()
    gone = fall.at[pl.ds(0, 7), pl.ds(0, 784)]
    remote(gone, gone, ring_s, ring_r.at[0, 0], partner).wait_send()
    gone = sendb.at[:, :, pl.ds(0, NXY - 1)]
    remote(gone, gone, ex_s, ex_r.at[0], partner).wait_send()
    code_all(7, 0).wait_send()
    store_agg.wait()
    store.wait()
    last.wait()


def finish(agg_in, wgrad_in, agg, wgrad):
    agg[...] = agg_in[...]
    wgrad[...] = wgrad_in[0:SHARD]


def shards(features, cotangent, wigner, src_atom, dst_part, dst_atom, angle, w_zero, w_one, w_two):
    dma = pltpu.SemaphoreType.DMA
    scratch = [
        pltpu.VMEM((49, ATOMS, 128), BF),
        pltpu.VMEM((49, KEPT, 256), BF),
        pltpu.VMEM(w_zero.shape, BF),
        pltpu.VMEM(w_one.shape, BF),
        pltpu.VMEM(w_two.shape, BF),
        pltpu.VMEM((KEPT, SLOTS, 256), BF),
        pltpu.VMEM((KEPT, 64, 256), BF),
        pltpu.VMEM((KEPT, SLOTS, 256), BF),
        pltpu.VMEM((KEPT, SLOTS, 256), BF),
        pltpu.VMEM((NZ, 16, 128), BF),
        pltpu.VMEM((NZ, 3, 32, 128), BF),
        pltpu.VMEM((NZ, 832, 128), BF),
        pltpu.VMEM((832, 128), BF),
        pltpu.VMEM((NZ, WIRE, NXY, 2, 128), BF),
        pltpu.VMEM((WIRE, NZ, NXY, 2, 128), BF),
        pltpu.VMEM((KEPT, SLOTS, 128), BF),
        pltpu.VMEM((KEPT, 128, SLOTS), BF),
        pltpu.VMEM((ROWS + 24, 128), F32),
        pltpu.VMEM((128, HALF, 128), BF),
        pltpu.VMEM((128, HALF, 128), BF),
        pltpu.VMEM((2, 4, 4, NZ, RING, 128), BF),
    ]
    scratch += [pltpu.VMEM((2, 4, NZ, RING, 128), BF) for _ in range(4)]
    scratch += [pltpu.VMEM((2, 4, NZ, RING, 128), BF)]
    scratch += [pltpu.VMEM((2, NZ, RING, 128), BF) for _ in range(4)]
    scratch += [pltpu.VMEM((2, NZ, RING, 128), BF)]
    scratch += [
        pltpu.VMEM((2, NZ, RING, 128), BF),
        pltpu.VMEM((HALF, 128), F32),
        pltpu.VMEM((NZ, NXY, REST, 128), BF),
        pltpu.VMEM((4, 2, 8, REST, 128), BF),
        pltpu.VMEM((3, 2, 8, REST, 128), BF),
        pltpu.VMEM((3, 2, 8, REST, 128), BF),
        pltpu.VMEM((2, 2, 8, REST, 128), BF),
        pltpu.VMEM((NXY, REST, 128), BF),
        pltpu.VMEM((NXY, REST, 128), BF),
        dma, dma((3,)),
        dma, dma((7, 2)),
        dma, dma((2,)), dma((2,)),
        dma, dma((3,)),
        dma, dma((2, 9)),
        dma, dma((2, 3)),
        dma, dma((2,)),
        dma, dma,
        dma((6,)), dma((2,)),
        dma, dma((4, 2)), dma, dma((3, 2)), dma, dma,
    ]
    vmem = pl.BlockSpec(memory_space=pltpu.VMEM)
    agg, wgrad = pl.pallas_call(
        kernel,
        out_shape=(
            jax.ShapeDtypeStruct((49, ATOMS, 128), BF),
            jax.ShapeDtypeStruct((2 * HALF, 128), F32),
        ),
        in_specs=[vmem] * 4 + [pl.BlockSpec(memory_space=pl.ANY)] * 6,
        out_specs=(pl.BlockSpec(memory_space=pl.ANY),) * 2,
        scratch_shapes=scratch,
        compiler_params=pltpu.CompilerParams(
            collective_id=0, has_side_effects=True, vmem_limit_bytes=67000000
        ),
    )(
        dst_part.reshape(1, EDGES),
        src_atom.reshape(1, EDGES),
        dst_atom.reshape(1, EDGES),
        angle.reshape(1, EDGES),
        jnp.transpose(wigner, (2, 1, 0)),
        jnp.transpose(features, (1, 0, 2)).reshape(784, 128),
        jnp.transpose(cotangent, (1, 0, 2)).reshape(784, 128),
        w_zero, w_one, w_two,
    )
    agg, wgrad = pl.pallas_call(
        finish,
        out_shape=(
            jax.ShapeDtypeStruct((49, ATOMS, 128), BF),
            jax.ShapeDtypeStruct((SHARD, 128), F32),
        ),
        in_specs=[vmem] * 2,
        out_specs=(vmem, vmem),
    )(agg, wgrad)
    return jnp.transpose(agg, (1, 0, 2)), wgrad.reshape(SHARD * 128)


def solution(mesh):
    both = ("dp", "graph")
    placed = (
        P(both, None, None), P(both, None, None), P(), P(both), P(both, None), P(both), P(both), P(), P(), P(),
    )
    return jax.shard_map(
        shards,
        mesh=mesh,
        in_specs=placed,
        out_specs=(P(both, None, None), P("graph")),
        check_vma=False,
    )
```

```python
import functools

import jax
import jax.numpy as jnp
from jax import lax
from jax.experimental import pallas as pl
from jax.experimental.pallas import tpu as pltpu
from jax.sharding import PartitionSpec as P

LMAX = 6
MMAX = 2
NX, NZ, NY = 4, 8, 4
NXY = NX * NY
EDGES = 128
ATOMS = 16
SLOTS = 256
ROWS = 21888
SHARD = 171
HALF = 88
RING = 32
REST = 24
MESH = pl.DeviceIdType.MESH
BF = jnp.bfloat16
F32 = jnp.float32


def kept_degrees():
    out = list(range(LMAX + 1))
    for m in range(1, MMAX + 1):
        for _ in range(2):
            out.extend(range(m, LMAX + 1))
    return out


DEGREE = kept_degrees()
KEPT = len(DEGREE)
WIRE = KEPT + 1
SPLIT = 20
CODE = SPLIT - 1
BY_DEGREE = sorted(range(KEPT), key=lambda k: (DEGREE[k], k))
PLACE = {k: i if i < CODE else i + 1 for i, k in enumerate(BY_DEGREE)}
GROUPS = [(0, 7), (7, 6), (13, 6), (19, 5), (24, 5)]


def width(degree):
    return 128 if degree <= 3 else 256


def dot(a, b):
    return jnp.dot(a, b, preferred_element_type=F32)


def iota(shape, dim):
    return lax.broadcasted_iota(jnp.int32, shape, dim)


def remote(src, dst, send, recv, device):
    return pltpu.make_async_remote_copy(
        src_ref=src, dst_ref=dst, send_sem=send, recv_sem=recv, device_id=device, device_id_type=MESH
    )


def build_table(wig, wk, table):
    wk[...] = jnp.zeros_like(wk)
    wk[:, 0:49, :] = jnp.swapaxes(wig[...].astype(F32), 0, 1).astype(BF)
    for degree in range(LMAX + 1):
        w = width(degree)
        j = iota((w, 64), 1)
        n = iota((w, 64), 0)
        spread = ((j == degree * degree + n // ATOMS) & (n < ATOMS * (2 * degree + 1))).astype(BF)
        for k in [k for k in range(KEPT) if DEGREE[k] == degree]:
            table[k, 0:w] = dot(spread, wk[k]).astype(BF)


def build_rotation(angle, atom, table, left, rows):
    size = angle.shape[0]
    lane = iota((size, 128), 1)
    near = (angle == lane.astype(F32)).astype(BF)
    far = (angle == (lane + 128).astype(F32)).astype(BF)
    pick = jnp.concatenate([near, far], axis=1)
    mask = (atom == (lane % ATOMS + 1).astype(F32)).astype(F32)
    wide = jnp.concatenate([mask, mask], axis=1)
    for k in range(KEPT):
        w = width(DEGREE[k])
        gate = mask if w == 128 else wide
        got = lax.dot_general(pick, table[k, 0:w], (((1,), (1,)), ((), ())), preferred_element_type=F32)
        got = (got * gate).astype(BF)
        step = size // len(rows)
        for i, part in enumerate(rows):
            left[k, part, 0:w] = got[step * i : step * i + step]


def kernel(
    tgt, src, dat, ang, wig_in, feat, cot, w0_in, w1_in, w2_in,
    agg_out, wgrad,
    agg, wig, w0, w1, w2, table, wk, left, leftd, crow, codes, fall, cpad, sendb, recvb, pull, xt, flat,
    pk, r0, s0, ra, ta, rb, rc, s1, ra1, ta1, rb1, rc1, s2, r3, fin,
    sz, ua, va, ub, vb, sz1, r4,
    code_s, code_r, ring_s, ring_r, ex_s, ex_r, loc_s, dp_s, dp_r, st_s, st_r, su_s, su_r, z_s, z_r, f_s, f_r, in_s, out_s,
    ua_s, ua_r, ub_s, ub_r, w_s, w_r,
):
    dp = lax.axis_index("dp")
    g = lax.axis_index("graph")
    x = g // 32
    z = (g // 4) % 8
    y = g % 4
    xy = x * 4 + y
    sign = 1 - 2 * dp

    def at(px, pz, py):
        return (dp, px * 32 + pz * 4 + py)

    partner = (1 - dp, g)

    def zpeer(i):
        return lax.rem(z + i, NZ)

    def xypeer(i):
        return lax.rem(xy + i, NXY)

    loads = [
        pltpu.make_async_copy(a, b, in_s.at[i])
        for i, (a, b) in enumerate(
            [
                (wig_in, wig), (feat, fall.at[z, pl.ds(0, 784)]), (cot, cpad.at[pl.ds(0, 784)]),
                (w0_in, w0), (w1_in, w1), (w2_in, w2),
            ]
        )
    ]
    loads[1].start()

    barrier = pltpu.get_barrier_semaphore()

    def greet_z(i, c):
        pl.semaphore_signal(barrier, inc=1, device_id=at(x, zpeer(i), y), device_id_type=MESH)
        return c

    def greet_xy(i, c):
        q = xypeer(i)
        pl.semaphore_signal(barrier, inc=1, device_id=at(q // 4, z, q % 4), device_id_type=MESH)
        return c

    lax.fori_loop(1, NZ, greet_z, 0)
    lax.fori_loop(1, NXY, greet_xy, 0)
    pl.semaphore_signal(barrier, inc=1, device_id=partner, device_id_type=MESH)

    for load in loads[:3:2]:
        load.start()

    trow = jnp.broadcast_to(tgt[...], (EDGES, EDGES)).astype(F32)
    tcol = jnp.transpose(trow)
    earlier = (tcol == trow) & (iota((EDGES, EDGES), 0) < iota((EDGES, EDGES), 1))
    rank = jnp.sum(earlier.astype(F32), axis=0, keepdims=True).astype(jnp.int32)
    t = tgt[...]
    pos = ((t >> 2) & 7) * 32 + ((t >> 5) * 4 + (t & 3)) * 2 + rank
    line = iota((16, EDGES), 0)
    code = jnp.zeros((16, EDGES), jnp.int32)
    for i, row in enumerate([pos, ang[...], src[...] + 1, dat[...] + 1]):
        code = jnp.where(line == i, jnp.broadcast_to(row, (16, EDGES)), code)
    crow[z] = code.astype(F32).astype(BF)

    def expand(q):
        c = crow[q].astype(F32)
        hot = (iota((32, EDGES), 0) + 32 * z).astype(F32) == jnp.broadcast_to(c[0:1], (32, EDGES))
        wide = jnp.concatenate([jnp.broadcast_to(c[i : i + 1], (EDGES, EDGES)) for i in (1, 2, 3)], axis=0)
        got = lax.dot_general(
            hot.astype(BF), wide.astype(BF), (((1,), (1,)), ((), ())), preferred_element_type=F32
        )
        codes[q, 0] = got[:, 0:128].astype(BF)
        codes[q, 1] = got[:, 128:256].astype(BF)
        codes[q, 2] = jnp.where(iota((32, 128), 1) < 64, got[:, 0:128], got[:, 256:384]).astype(BF)

    for q in range(NZ):
        fall[q, 784:832] = jnp.zeros((48, 128), BF)

    def exchange(step, piece, i):
        q = xypeer(i)
        part = pl.ds(0, SPLIT) if piece == 0 else pl.ds(SPLIT, WIRE - SPLIT)
        return remote(
            sendb.at[step, part, q], recvb.at[part, step, xy], ex_s, ex_r.at[step // 4], at(q // 4, z, q % 4)
        )

    def own_copy(step):
        return pltpu.make_async_copy(sendb.at[step, :, xy], recvb.at[:, step, xy], loc_s.at[step // 4])

    def rotate(step, piece, zz):
        rows = pl.ds(pl.multiple_of(zz * 32, 32), 32)
        for degree in range(5) if piece == 0 else range(5, LMAX + 1):
            w = width(degree)
            ks = [k for k in range(KEPT) if DEGREE[k] == degree]
            lhs = jnp.concatenate([left[k, rows, 0:w] for k in ks], axis=0)
            lo = ATOMS * degree * degree
            if piece == 0:
                w = min(w, 400 - lo)
                lhs = lhs[:, 0:w]
            got = dot(lhs, fall[zz, lo : lo + w]).astype(BF)
            for i, k in enumerate(ks):
                sendb[step, PLACE[k]] = got[32 * i : 32 * i + 32].reshape(NXY, 2, 128)
        if piece == 0:
            sendb[step, CODE] = codes[zz, 2].reshape(NXY, 2, 128)

    def send_block(step, piece):
        def go(h, c):
            for i in range(1, 6):
                exchange(step, piece, 5 * h + i).start()
            return c

        lax.fori_loop(0, 3, go, 0)
        if piece:
            own_copy(step).start()

    def receive_half(h):
        part = recvb.at[:, pl.ds(4 * h, 4), pl.ds(0, NXY - 1)]
        remote(part, part, ex_s, ex_r.at[h], partner).wait_recv()
        part = recvb.at[:, pl.ds(4 * h, 4), 0]
        pltpu.make_async_copy(part, part, loc_s.at[h]).wait()

    loads[1].wait()
    pl.semaphore_wait(barrier, 23)

    def code_copy(i):
        lane = 0 if i == 1 else 1 if i == NZ - 1 else 2
        return remote(crow.at[z], crow.at[z], code_s, code_r.at[lane], at(x, zpeer(i), y))

    def code_all(count, lane):
        part = crow.at[pl.ds(0, count)]
        return remote(part, part, code_s, code_r.at[lane], partner)

    for i in range(1, NZ):
        code_copy(i).start()

    def ring(hop, piece, block, direction):
        dev = at(x, lax.rem(z + direction + NZ, NZ), y)
        part = fall.at[block, pl.ds(400 * piece, 400 - 16 * piece)]
        return remote(part, part, ring_s, ring_r.at[hop, piece], dev)

    def behind(n):
        return lax.rem(z - sign * n + 2 * NZ, NZ)

    def ahead(n):
        return lax.rem(z + sign * n + 2 * NZ, NZ)

    for piece in range(2):
        ring(0, piece, z, sign).start()
    loads[0].wait()
    build_table(wig, wk, table)
    for piece in range(2):
        ring(4, piece, z, -sign).start()
    expand(z)
    mine = pl.ds(pl.multiple_of(z * 32, 32), 32)
    build_rotation(codes[z, 0].astype(F32), codes[z, 1].astype(F32), table, left, [mine])
    for piece in range(2):
        rotate(0, piece, z)
        send_block(0, piece)
    for load in loads[3:]:
        load.start()
    cpad[784:832] = jnp.zeros((48, 128), BF)

    def prepare(blocks):
        for q in blocks:
            expand(q)
        rows = [pl.ds(pl.multiple_of(q * 32, 32), 32) for q in blocks]
        build_rotation(
            jnp.concatenate([codes[q, 0] for q in blocks], axis=0).astype(F32),
            jnp.concatenate([codes[q, 1] for q in blocks], axis=0).astype(F32),
            table, left, rows,
        )

    def half(h):
        rows = pl.ds(128 * h, 128)

        def rot(k):
            return recvb[k, 4 * h : 4 * h + 4].reshape(128, 128)

        r, c = iota((128, 256), 0), iota((128, 256), 1)
        parted = dot(rot(CODE), (r == jnp.where(c < 128, 0, 64)).astype(BF))
        build_rotation(parted[:, 0:128], parted[:, 128:256], table, leftd, [rows])
        for k in range(KEPT):
            w = width(DEGREE[k])
            lo = ATOMS * DEGREE[k] * DEGREE[k]
            pull[k, rows] = dot(leftd[k, rows, 0:w], cpad[lo : lo + w]).astype(BF)
            xt[k, :, rows] = jnp.transpose(rot(PLACE[k]).astype(F32)).astype(BF)

    def pass_on(n, piece, back):
        if back:
            ring(n - 1, piece, behind(n), sign).wait_recv()
            if n < 4:
                ring(n, piece, behind(n), sign).start()
        elif n < 4:
            ring(3 + n, piece, ahead(n), -sign).wait_recv()
            if n < 3:
                ring(4 + n, piece, ahead(n), -sign).start()

    code_all(1, 0).wait_recv()
    code_all(1, 1).wait_recv()
    prepare([behind(1), ahead(1)])
    for n in range(1, 5):
        for back in (True, False):
            if n == 4 and not back:
                break
            step = 2 * n - 1 if back else 2 * n
            for piece in range(2):
                pass_on(n, piece, back)
                if n == 2 and back and piece == 0:
                    code_all(5, 2).wait_recv()
                    prepare([behind(2), ahead(2), behind(3), ahead(3), behind(4)])
                rotate(step, piece, behind(n) if back else ahead(n))
                send_block(step, piece)
    loads[2].wait()
    receive_half(0)
    half(0)
    receive_half(1)
    half(1)

    def spread(res, base, length, lo, width_):
        for jb in range(lo, lo + width_):
            flat[pl.ds(base + jb, 128 * length, stride=length), :] = res[:, 128 * (jb - lo) : 128 * (jb - lo) + 128]

    def grads(m):
        if m == 0:
            zt = jnp.concatenate([xt[k] for k in range(7)], axis=0)
            for lo in range(0, 7, 2):
                n = min(2, 7 - lo)
                rhs = jnp.concatenate([pull[lo + i] for i in range(n)], axis=1)
                spread(dot(zt, rhs), 0, 7, lo, n)
            return
        base = 128 * (49 if m == 1 else 49 + 72)
        plus, length = GROUPS[2 * m - 1]
        minus = GROUPS[2 * m][0]
        pqt = jnp.concatenate(
            [jnp.concatenate([xt[plus + i], xt[minus + i]], axis=1) for i in range(length)], axis=0
        )
        for lo in range(0, length, 2):
            n = min(2, length - lo)
            gg = jnp.concatenate([pull[plus + lo + i] for i in range(n)], axis=1)
            hh = jnp.concatenate([pull[minus + lo + i] for i in range(n)], axis=1)
            spread(dot(pqt, jnp.concatenate([gg, hh], axis=0)), base, length, lo, n)
            spread(dot(pqt, jnp.concatenate([hh, -gg], axis=0)), base + 128 * length * length, length, lo, n)

    def pack(s, c):
        pk[s] = flat[pl.ds(SHARD * s + HALF * (1 - dp), HALF), :].astype(BF)
        return c

    def merge(s, c):
        sx = s // 32
        cz = (s // 4) % 8
        sy = s % 4
        both = (flat[pl.ds(SHARD * s + HALF * dp, HALF), :] + r0[s].astype(F32)).astype(BF)
        s0[0, sx, sy, cz] = both[0:RING]
        s0[1, sy, sx, cz] = both[RING : 2 * RING]
        sz[cz, sx * 4 + sy] = both[2 * RING : HALF]
        return c

    flat[ROWS : ROWS + 24] = jnp.zeros((24, 128), F32)
    runs = [(0, 36), (36, 90), (90, 128)]
    swaps = []
    for m, (lo, hi) in enumerate(runs):
        grads(m)
        lax.fori_loop(lo // 2, hi // 2, lambda h, c: pack(2 * h + 1, pack(2 * h, c)), 0)
        part = pl.ds(lo, hi - lo)
        swaps.append(remote(pk.at[part], r0.at[part], dp_s, dp_r.at[m], partner))
        swaps[m].start()
    for m, (lo, hi) in enumerate(runs):
        swaps[m].wait_recv()
        lax.fori_loop(lo // 2, hi // 2, lambda h, c: merge(2 * h + 1, merge(2 * h, c)), 0)

    def mixed(k):
        return recvb[k].reshape(SLOTS, 128)

    def cat(ks):
        return jnp.concatenate([mixed(PLACE[k]) for k in ks], axis=1)

    message = {}

    def mix(m):
        if m == 0:
            zero = dot(cat(range(7)), w0[...]).astype(BF)
            for i in range(7):
                message[i] = zero[:, 128 * i : 128 * i + 128]
            return
        w = w1 if m == 1 else w2
        plus, length = GROUPS[2 * m - 1]
        minus = GROUPS[2 * m][0]
        p, q = cat(range(plus, plus + length)), cat(range(minus, minus + length))
        up = (dot(p, w[0]) - dot(q, w[1])).astype(BF)
        um = (dot(p, w[1]) + dot(q, w[0])).astype(BF)
        for i in range(length):
            message[plus + i] = up[:, 128 * i : 128 * i + 128]
            message[minus + i] = um[:, 128 * i : 128 * i + 128]

    def gather_atoms():
        for degree in range(LMAX + 1):
            w = width(degree)
            ks = [k for k in range(KEPT) if DEGREE[k] == degree]
            lhs = jnp.concatenate([leftd[k, :, 0:w] for k in ks], axis=0)
            rhs = jnp.concatenate([message[k] for k in ks], axis=0)
            got = lax.dot_general(lhs, rhs, (((0,), (0,)), ((), ())), preferred_element_type=F32)
            size = 2 * degree + 1
            agg[degree * degree : (degree + 1) * (degree + 1)] = (
                got[0 : ATOMS * size].astype(BF).reshape(size, ATOMS, 128)
            )

    def along_x(d):
        return at(lax.rem(x + d + NX, NX), z, y)

    def along_y(d):
        return at(x, z, lax.rem(y + d + NY, NY))

    def mod4(v):
        return lax.rem(v + 4, 4)

    parts = [(0, x, along_x, y, along_y), (1, y, along_y, x, along_x)]
    one, two, three, subs = [], [], [], []
    for i, p, move, q, _ in parts:
        order = [mod4(q + 2 * sign), mod4(q - sign), mod4(q + sign), q]
        subs.append(order)
        one.append(
            [remote(s0.at[i, mod4(p + 2 * sign), j], ra.at[i, j], st_s, st_r.at[i, n], move(sign))
             for n, j in enumerate(order)]
        )
        two.append(
            [remote(s0.at[i, mod4(p - sign), j], rb.at[i, j], st_s, st_r.at[i, 8], move(-sign))
             for n, j in enumerate(order)]
        )
        three.append(
            [remote(ta.at[i, j], rc.at[i, j], st_s, st_r.at[i, 4 + n], move(sign))
             for n, j in enumerate(order)]
        )
    def mod8(v):
        return lax.rem(v + 8, 8)

    def up(h, j):
        src = sz.at[mod8(z + 4 * sign), pl.ds(8 * j, 8)] if h == 0 else va.at[h - 1, j]
        return remote(src, ua.at[h, j], ua_s, ua_r.at[h, j], at(x, mod8(z + sign), y))

    def down(h, j):
        src = sz.at[mod8(z - 3 * sign), pl.ds(8 * j, 8)] if h == 0 else vb.at[h - 1, j]
        return remote(src, ub.at[h, j], ub_s, ub_r.at[h, j], at(x, mod8(z - sign), y))

    def pass_sum(h, j):
        part = pl.ds(8 * j, 8)
        up(h, j).wait_recv()
        va[h, j] = (ua[h, j].astype(F32) + sz[mod8(z + (3 - h) * sign), part].astype(F32)).astype(BF)
        up(h + 1, j).start()
        if h < 2:
            down(h, j).wait_recv()
            vb[h, j] = (ub[h, j].astype(F32) + sz[mod8(z - (2 - h) * sign), part].astype(F32)).astype(BF)
            down(h + 1, j).start()

    def end_sum(j):
        part = pl.ds(8 * j, 8)
        up(3, j).wait_recv()
        down(2, j).wait_recv()
        sz1[part] = (sz[z, part].astype(F32) + ua[3, j].astype(F32) + ub[2, j].astype(F32)).astype(BF)

    def relay(n):
        for i, p, *_ in parts:
            j = subs[i][n]
            one[i][n].wait_recv()
            ta[i, j] = (ra[i, j].astype(F32) + s0[i, mod4(p + sign), j].astype(F32)).astype(BF)
            three[i][n].start()

    four, five, six = [], [], []
    for i, p, _, q, move in parts:
        order = subs[i]
        four.append(remote(s1.at[i, order[0]], ra1.at[i], su_s, su_r.at[i, 0], move(sign)))
        five.append(remote(s1.at[i, order[1]], rb1.at[i], su_s, su_r.at[i, 1], move(-sign)))
        six.append(remote(ta1.at[i], rc1.at[i], su_s, su_r.at[i, 2], move(sign)))

    def close(n):
        for i, p, *_ in parts:
            j = subs[i][n]
            if n == 0:
                remote(rb.at[i], rb.at[i], st_s, st_r.at[i, 8], partner).wait_recv()
            three[i][n].wait_recv()
            s1[i, j] = (s0[i, p, j].astype(F32) + rb[i, j].astype(F32) + rc[i, j].astype(F32)).astype(BF)
            if n == 0:
                four[i].start()
            if n == 1:
                five[i].start()

    for j in range(2):
        up(0, j).start()
        down(0, j).start()
    for n in range(4):
        for i in range(2):
            one[i][n].start()
            two[i][n].start()
    for load in loads[3:]:
        load.wait()
    mix(1)
    mix(2)
    pass_sum(0, 0)
    relay(0)
    pass_sum(0, 1)
    relay(1)
    mix(0)
    pass_sum(1, 0)
    relay(2)
    pass_sum(1, 1)
    relay(3)
    pass_sum(2, 0)
    close(0)
    pass_sum(2, 1)
    for n in range(1, 4):
        close(n)
    for i in range(2):
        four[i].wait_recv()
        ta1[i] = (ra1[i].astype(F32) + s1[i, subs[i][2]].astype(F32)).astype(BF)
        six[i].start()
    for j in range(2):
        end_sum(j)

    def across(i):
        q = xypeer(i)
        return remote(sz1.at[q], r4.at[i], w_s, w_r, at(q // 4, z, q % 4))

    def across_go(i, c):
        across(i).start()
        return c

    lax.fori_loop(1, NXY, across_go, 0)
    def zcopy(a, i):
        q = zpeer(i)
        return remote(s2.at[a, q], r3.at[a, i], z_s, z_r.at[a], at(x, q, y))

    gather_atoms()
    store_agg = pltpu.make_async_copy(agg, agg_out, out_s.at[0])
    store_agg.start()
    for i in range(2):
        five[i].wait_recv()
        six[i].wait_recv()
        s2[i] = (s1[i, subs[i][3]].astype(F32) + rb1[i].astype(F32) + rc1[i].astype(F32)).astype(BF)
        for far in (4, 3, 5, 2, 6, 1, 7):
            zcopy(i, far).start()

    total = sz1[xy].astype(F32)
    part = r4.at[pl.ds(1, NXY - 1)]
    remote(part, part, w_s, w_r, partner).wait()
    for i in range(1, NXY):
        total = total + r4[i].astype(F32)
    fin[2 * RING : HALF] = total
    for a in range(2):
        total = s2[a, z].astype(F32)
        part = r3.at[a, pl.ds(1, NZ - 1)]
        remote(part, part, z_s, z_r.at[a], partner).wait_recv()
        for i in range(1, NZ):
            total = total + r3[a, i].astype(F32)
        fin[RING * a : RING * a + RING] = total
    mine = wgrad.at[pl.ds(pl.multiple_of(HALF * dp, 8), HALF)]
    last = remote(fin, mine, f_s, f_r, partner)
    last.start()
    store = pltpu.make_async_copy(fin, mine, out_s.at[1])
    store.start()
    for part, sem in (
        (ua, ua_s), (ub, ub_s), (s0.at[:, pl.ds(0, 3)], st_s), (s1.at[:, pl.ds(0, 3)], su_s),
        (s2.at[:, pl.ds(0, NZ - 1)], z_s), (pk, dp_s),
    ):
        remote(part, part, sem, f_r, partner).wait_send()
    gone = fall.at[pl.ds(0, 7), pl.ds(0, 784)]
    remote(gone, gone, ring_s, ring_r.at[0, 0], partner).wait_send()
    gone = sendb.at[:, :, pl.ds(0, NXY - 1)]
    remote(gone, gone, ex_s, ex_r.at[0], partner).wait_send()
    code_all(7, 0).wait_send()
    store_agg.wait()
    store.wait()
    last.wait()


def finish(agg_in, wgrad_in, agg, wgrad):
    agg[...] = agg_in[...]
    wgrad[...] = wgrad_in[0:SHARD]


def shards(features, cotangent, wigner, src_atom, dst_part, dst_atom, angle, w_zero, w_one, w_two):
    dma = pltpu.SemaphoreType.DMA
    scratch = [
        pltpu.VMEM((49, ATOMS, 128), BF),
        pltpu.VMEM((49, KEPT, 256), BF),
        pltpu.VMEM(w_zero.shape, BF),
        pltpu.VMEM(w_one.shape, BF),
        pltpu.VMEM(w_two.shape, BF),
        pltpu.VMEM((KEPT, SLOTS, 256), BF),
        pltpu.VMEM((KEPT, 64, 256), BF),
        pltpu.VMEM((KEPT, SLOTS, 256), BF),
        pltpu.VMEM((KEPT, SLOTS, 256), BF),
        pltpu.VMEM((NZ, 16, 128), BF),
        pltpu.VMEM((NZ, 3, 32, 128), BF),
        pltpu.VMEM((NZ, 832, 128), BF),
        pltpu.VMEM((832, 128), BF),
        pltpu.VMEM((NZ, WIRE, NXY, 2, 128), BF),
        pltpu.VMEM((WIRE, NZ, NXY, 2, 128), BF),
        pltpu.VMEM((KEPT, SLOTS, 128), BF),
        pltpu.VMEM((KEPT, 128, SLOTS), BF),
        pltpu.VMEM((ROWS + 24, 128), F32),
        pltpu.VMEM((128, HALF, 128), BF),
        pltpu.VMEM((128, HALF, 128), BF),
        pltpu.VMEM((2, 4, 4, NZ, RING, 128), BF),
    ]
    scratch += [pltpu.VMEM((2, 4, NZ, RING, 128), BF) for _ in range(4)]
    scratch += [pltpu.VMEM((2, 4, NZ, RING, 128), BF)]
    scratch += [pltpu.VMEM((2, NZ, RING, 128), BF) for _ in range(4)]
    scratch += [pltpu.VMEM((2, NZ, RING, 128), BF)]
    scratch += [
        pltpu.VMEM((2, NZ, RING, 128), BF),
        pltpu.VMEM((HALF, 128), F32),
        pltpu.VMEM((NZ, NXY, REST, 128), BF),
        pltpu.VMEM((4, 2, 8, REST, 128), BF),
        pltpu.VMEM((3, 2, 8, REST, 128), BF),
        pltpu.VMEM((3, 2, 8, REST, 128), BF),
        pltpu.VMEM((2, 2, 8, REST, 128), BF),
        pltpu.VMEM((NXY, REST, 128), BF),
        pltpu.VMEM((NXY, REST, 128), BF),
        dma, dma((3,)),
        dma, dma((7, 2)),
        dma, dma((2,)), dma((2,)),
        dma, dma((3,)),
        dma, dma((2, 9)),
        dma, dma((2, 3)),
        dma, dma((2,)),
        dma, dma,
        dma((6,)), dma((2,)),
        dma, dma((4, 2)), dma, dma((3, 2)), dma, dma,
    ]
    vmem = pl.BlockSpec(memory_space=pltpu.VMEM)
    agg, wgrad = pl.pallas_call(
        kernel,
        out_shape=(
            jax.ShapeDtypeStruct((49, ATOMS, 128), BF),
            jax.ShapeDtypeStruct((2 * HALF, 128), F32),
        ),
        in_specs=[vmem] * 4 + [pl.BlockSpec(memory_space=pl.ANY)] * 6,
        out_specs=(pl.BlockSpec(memory_space=pl.ANY),) * 2,
        scratch_shapes=scratch,
        compiler_params=pltpu.CompilerParams(
            collective_id=0, has_side_effects=True, vmem_limit_bytes=67000000
        ),
    )(
        dst_part.reshape(1, EDGES),
        src_atom.reshape(1, EDGES),
        dst_atom.reshape(1, EDGES),
        angle.reshape(1, EDGES),
        jnp.transpose(wigner, (2, 1, 0)),
        jnp.transpose(features, (1, 0, 2)).reshape(784, 128),
        jnp.transpose(cotangent, (1, 0, 2)).reshape(784, 128),
        w_zero, w_one, w_two,
    )
    agg, wgrad = pl.pallas_call(
        finish,
        out_shape=(
            jax.ShapeDtypeStruct((49, ATOMS, 128), BF),
            jax.ShapeDtypeStruct((SHARD, 128), F32),
        ),
        in_specs=[vmem] * 2,
        out_specs=(vmem, vmem),
    )(agg, wgrad)
    return jnp.transpose(agg, (1, 0, 2)), wgrad.reshape(SHARD * 128)


def solution(mesh):
    both = ("dp", "graph")
    placed = (
        P(both, None, None), P(both, None, None), P(), P(both), P(both, None), P(both), P(both), P(), P(), P(),
    )
    return jax.shard_map(
        shards,
        mesh=mesh,
        in_specs=placed,
        out_specs=(P(both, None, None), P("graph")),
        check_vma=False,
    )
```

```python
import functools

import jax
import jax.numpy as jnp
from jax import lax
from jax.experimental import pallas as pl
from jax.experimental.pallas import tpu as pltpu
from jax.sharding import PartitionSpec as P

LMAX = 6
MMAX = 2
NX, NZ, NY = 4, 8, 4
NXY = NX * NY
EDGES = 128
ATOMS = 16
SLOTS = 256
ROWS = 21888
SHARD = 171
HALF = 88
RING = 32
REST = 24
MESH = pl.DeviceIdType.MESH
BF = jnp.bfloat16
F32 = jnp.float32


def kept_degrees():
    out = list(range(LMAX + 1))
    for m in range(1, MMAX + 1):
        for _ in range(2):
            out.extend(range(m, LMAX + 1))
    return out


DEGREE = kept_degrees()
KEPT = len(DEGREE)
WIRE = KEPT + 1
SPLIT = 20
CODE = SPLIT - 1
BY_DEGREE = sorted(range(KEPT), key=lambda k: (DEGREE[k], k))
PLACE = {k: i if i < CODE else i + 1 for i, k in enumerate(BY_DEGREE)}
GROUPS = [(0, 7), (7, 6), (13, 6), (19, 5), (24, 5)]


def width(degree):
    return 128 if degree <= 3 else 256


def dot(a, b):
    return jnp.dot(a, b, preferred_element_type=F32)


def iota(shape, dim):
    return lax.broadcasted_iota(jnp.int32, shape, dim)


def remote(src, dst, send, recv, device):
    return pltpu.make_async_remote_copy(
        src_ref=src, dst_ref=dst, send_sem=send, recv_sem=recv, device_id=device, device_id_type=MESH
    )


def build_table(wig, wk, table):
    wk[:, 48:64] = jnp.zeros((KEPT, 16, 256), BF)
    wk[:, 0:49, :] = jnp.swapaxes(wig[...].astype(F32), 0, 1).astype(BF)
    for degree in range(LMAX + 1):
        w = width(degree)
        j = iota((w, 64), 1)
        n = iota((w, 64), 0)
        spread = ((j == degree * degree + n // ATOMS) & (n < ATOMS * (2 * degree + 1))).astype(BF)
        for k in [k for k in range(KEPT) if DEGREE[k] == degree]:
            table[k, 0:w] = dot(spread, wk[k]).astype(BF)


def build_rotation(angle, atom, table, left, rows):
    size = angle.shape[0]
    lane = iota((size, 128), 1)
    near = (angle == lane.astype(F32)).astype(BF)
    far = (angle == (lane + 128).astype(F32)).astype(BF)
    pick = jnp.concatenate([near, far], axis=1)
    mask = (atom == (lane % ATOMS + 1).astype(F32)).astype(F32)
    wide = jnp.concatenate([mask, mask], axis=1)
    for k in range(KEPT):
        w = width(DEGREE[k])
        gate = mask if w == 128 else wide
        got = lax.dot_general(pick, table[k, 0:w], (((1,), (1,)), ((), ())), preferred_element_type=F32)
        got = (got * gate).astype(BF)
        step = size // len(rows)
        for i, part in enumerate(rows):
            left[k, part, 0:w] = got[step * i : step * i + step]


def kernel(
    tgt, src, dat, ang, wig_in, feat, cot, w0_in, w1_in, w2_in,
    agg_out, wgrad,
    agg, wig, w0, w1, w2, table, wk, left, leftd, crow, codes, fall, cpad, sendb, recvb, pull, xt, flat,
    pk, r0, s0, ra, ta, rb, rc, s1, ra1, ta1, rb1, rc1, s2, r3, fin,
    sz, ua, va, ub, vb, sz1, r4,
    code_s, code_r, ring_s, ring_r, ex_s, ex_r, loc_s, dp_s, dp_r, st_s, st_r, su_s, su_r, z_s, z_r, f_s, f_r, in_s, out_s,
    ua_s, ua_r, ub_s, ub_r, w_s, w_r,
):
    dp = lax.axis_index("dp")
    g = lax.axis_index("graph")
    x = g // 32
    z = (g // 4) % 8
    y = g % 4
    xy = x * 4 + y
    sign = 1 - 2 * dp

    def at(px, pz, py):
        return (dp, px * 32 + pz * 4 + py)

    partner = (1 - dp, g)

    def zpeer(i):
        return lax.rem(z + i, NZ)

    def xypeer(i):
        return lax.rem(xy + i, NXY)

    loads = [
        pltpu.make_async_copy(a, b, in_s.at[i])
        for i, (a, b) in enumerate(
            [
                (wig_in, wig), (feat, fall.at[z, pl.ds(0, 784)]), (cot, cpad.at[pl.ds(0, 784)]),
                (w0_in, w0), (w1_in, w1), (w2_in, w2),
            ]
        )
    ]
    loads[1].start()

    barrier = pltpu.get_barrier_semaphore()

    def greet_xy(h, c):
        for i in range(1, 6):
            q = xypeer(5 * h + i)
            pl.semaphore_signal(barrier, inc=1, device_id=at(q // 4, z, q % 4), device_id_type=MESH)
        return c

    for i in (4, 3, 5, 2, 6, 1, 7):
        pl.semaphore_signal(barrier, inc=1, device_id=at(x, zpeer(i), y), device_id_type=MESH)
    lax.fori_loop(0, 3, greet_xy, 0)
    pl.semaphore_signal(barrier, inc=1, device_id=partner, device_id_type=MESH)

    for load in loads[:3:2]:
        load.start()

    trow = jnp.broadcast_to(tgt[...], (EDGES, EDGES)).astype(F32)
    tcol = jnp.transpose(trow)
    earlier = (tcol == trow) & (iota((EDGES, EDGES), 0) < iota((EDGES, EDGES), 1))
    rank = jnp.sum(earlier.astype(F32), axis=0, keepdims=True).astype(jnp.int32)
    t = tgt[...]
    pos = ((t >> 2) & 7) * 32 + ((t >> 5) * 4 + (t & 3)) * 2 + rank
    line = iota((16, EDGES), 0)
    code = jnp.zeros((16, EDGES), jnp.int32)
    for i, row in enumerate([pos, ang[...], src[...] + 1, dat[...] + 1]):
        code = jnp.where(line == i, jnp.broadcast_to(row, (16, EDGES)), code)
    crow[z] = code.astype(F32).astype(BF)

    def expand(q):
        c = crow[q].astype(F32)
        hot = (iota((32, EDGES), 0) + 32 * z).astype(F32) == jnp.broadcast_to(c[0:1], (32, EDGES))
        wide = jnp.concatenate([jnp.broadcast_to(c[i : i + 1], (EDGES, EDGES)) for i in (1, 2, 3)], axis=0)
        got = lax.dot_general(
            hot.astype(BF), wide.astype(BF), (((1,), (1,)), ((), ())), preferred_element_type=F32
        )
        codes[q, 0] = got[:, 0:128].astype(BF)
        codes[q, 1] = got[:, 128:256].astype(BF)
        codes[q, 2] = jnp.where(iota((32, 128), 1) < 64, got[:, 0:128], got[:, 256:384]).astype(BF)

    for q in range(NZ):
        fall[q, 784:832] = jnp.zeros((48, 128), BF)

    def exchange(step, piece, i):
        q = xypeer(i)
        part = pl.ds(0, SPLIT) if piece == 0 else pl.ds(SPLIT, WIRE - SPLIT)
        return remote(
            sendb.at[step, part, q], recvb.at[part, step, xy], ex_s, ex_r.at[step // 4], at(q // 4, z, q % 4)
        )

    def own_copy(step):
        return pltpu.make_async_copy(sendb.at[step, :, xy], recvb.at[:, step, xy], loc_s.at[step // 4])

    def rotate(step, piece, zz):
        rows = pl.ds(pl.multiple_of(zz * 32, 32), 32)
        for degree in range(5) if piece == 0 else range(5, LMAX + 1):
            w = width(degree)
            ks = [k for k in range(KEPT) if DEGREE[k] == degree]
            lhs = jnp.concatenate([left[k, rows, 0:w] for k in ks], axis=0)
            lo = ATOMS * degree * degree
            if piece == 0:
                w = min(w, 400 - lo)
                lhs = lhs[:, 0:w]
            got = dot(lhs, fall[zz, lo : lo + w]).astype(BF)
            for i, k in enumerate(ks):
                sendb[step, PLACE[k]] = got[32 * i : 32 * i + 32].reshape(NXY, 2, 128)
        if piece == 0:
            sendb[step, CODE] = codes[zz, 2].reshape(NXY, 2, 128)

    def send_block(step, piece):
        def go(h, c):
            for i in range(1, 6):
                exchange(step, piece, 5 * h + i).start()
            return c

        lax.fori_loop(0, 3, go, 0)
        if piece:
            own_copy(step).start()

    def receive_half(h):
        part = recvb.at[:, pl.ds(4 * h, 4), pl.ds(0, NXY - 1)]
        remote(part, part, ex_s, ex_r.at[h], partner).wait_recv()
        part = recvb.at[:, pl.ds(4 * h, 4), 0]
        pltpu.make_async_copy(part, part, loc_s.at[h]).wait()

    loads[1].wait()
    pl.semaphore_wait(barrier, 23)

    def code_copy(i):
        lane = 0 if i == 1 else 1 if i == NZ - 1 else 2
        return remote(crow.at[z], crow.at[z], code_s, code_r.at[lane], at(x, zpeer(i), y))

    def code_all(count, lane):
        part = crow.at[pl.ds(0, count)]
        return remote(part, part, code_s, code_r.at[lane], partner)

    for i in range(1, NZ):
        code_copy(i).start()

    def ring(hop, piece, block, direction):
        dev = at(x, lax.rem(z + direction + NZ, NZ), y)
        part = fall.at[block, pl.ds(400 * piece, 400 - 16 * piece)]
        return remote(part, part, ring_s, ring_r.at[hop, piece], dev)

    def behind(n):
        return lax.rem(z - sign * n + 2 * NZ, NZ)

    def ahead(n):
        return lax.rem(z + sign * n + 2 * NZ, NZ)

    for piece in range(2):
        ring(0, piece, z, sign).start()
    loads[0].wait()
    build_table(wig, wk, table)
    for piece in range(2):
        ring(4, piece, z, -sign).start()
    expand(z)
    mine = pl.ds(pl.multiple_of(z * 32, 32), 32)
    build_rotation(codes[z, 0].astype(F32), codes[z, 1].astype(F32), table, left, [mine])
    for piece in range(2):
        rotate(0, piece, z)
        send_block(0, piece)
    for load in loads[3:]:
        load.start()
    cpad[784:832] = jnp.zeros((48, 128), BF)

    def prepare(blocks):
        for q in blocks:
            expand(q)
        rows = [pl.ds(pl.multiple_of(q * 32, 32), 32) for q in blocks]
        build_rotation(
            jnp.concatenate([codes[q, 0] for q in blocks], axis=0).astype(F32),
            jnp.concatenate([codes[q, 1] for q in blocks], axis=0).astype(F32),
            table, left, rows,
        )

    def half(h):
        rows = pl.ds(128 * h, 128)

        def rot(k):
            return recvb[k, 4 * h : 4 * h + 4].reshape(128, 128)

        r, c = iota((128, 256), 0), iota((128, 256), 1)
        parted = dot(rot(CODE), (r == jnp.where(c < 128, 0, 64)).astype(BF))
        build_rotation(parted[:, 0:128], parted[:, 128:256], table, leftd, [rows])
        for k in range(KEPT):
            w = width(DEGREE[k])
            lo = ATOMS * DEGREE[k] * DEGREE[k]
            pull[k, rows] = dot(leftd[k, rows, 0:w], cpad[lo : lo + w]).astype(BF)
            xt[k, :, rows] = jnp.transpose(rot(PLACE[k]).astype(F32)).astype(BF)

    def pass_on(n, piece, back):
        if back:
            ring(n - 1, piece, behind(n), sign).wait_recv()
            if n < 4:
                ring(n, piece, behind(n), sign).start()
        elif n < 4:
            ring(3 + n, piece, ahead(n), -sign).wait_recv()
            if n < 3:
                ring(4 + n, piece, ahead(n), -sign).start()

    code_all(1, 0).wait_recv()
    code_all(1, 1).wait_recv()
    prepare([behind(1), ahead(1)])
    for n in range(1, 5):
        for back in (True, False):
            if n == 4 and not back:
                break
            step = 2 * n - 1 if back else 2 * n
            for piece in range(2):
                pass_on(n, piece, back)
                if n == 2 and back and piece == 0:
                    code_all(5, 2).wait_recv()
                    prepare([behind(2), ahead(2), behind(3), ahead(3), behind(4)])
                rotate(step, piece, behind(n) if back else ahead(n))
                send_block(step, piece)
    loads[2].wait()
    receive_half(0)
    half(0)
    receive_half(1)
    half(1)

    def spread(res, base, length, lo, width_):
        for jb in range(lo, lo + width_):
            flat[pl.ds(base + jb, 128 * length, stride=length), :] = res[:, 128 * (jb - lo) : 128 * (jb - lo) + 128]

    def grads(m):
        if m == 0:
            zt = jnp.concatenate([xt[k] for k in range(7)], axis=0)
            for lo in range(0, 7, 2):
                n = min(2, 7 - lo)
                rhs = jnp.concatenate([pull[lo + i] for i in range(n)], axis=1)
                spread(dot(zt, rhs), 0, 7, lo, n)
            return
        base = 128 * (49 if m == 1 else 49 + 72)
        plus, length = GROUPS[2 * m - 1]
        minus = GROUPS[2 * m][0]
        pqt = jnp.concatenate(
            [jnp.concatenate([xt[plus + i], xt[minus + i]], axis=1) for i in range(length)], axis=0
        )
        for lo in range(0, length, 2):
            n = min(2, length - lo)
            gg = jnp.concatenate([pull[plus + lo + i] for i in range(n)], axis=1)
            hh = jnp.concatenate([pull[minus + lo + i] for i in range(n)], axis=1)
            spread(dot(pqt, jnp.concatenate([gg, hh], axis=0)), base, length, lo, n)
            spread(dot(pqt, jnp.concatenate([hh, -gg], axis=0)), base + 128 * length * length, length, lo, n)

    def pack(s, c):
        pk[s] = flat[pl.ds(SHARD * s + HALF * (1 - dp), HALF), :].astype(BF)
        return c

    def merge(s, c):
        sx = s // 32
        cz = (s // 4) % 8
        sy = s % 4
        both = (flat[pl.ds(SHARD * s + HALF * dp, HALF), :] + r0[s].astype(F32)).astype(BF)
        s0[0, sx, sy, cz] = both[0:RING]
        s0[1, sy, sx, cz] = both[RING : 2 * RING]
        sz[cz, sx * 4 + sy] = both[2 * RING : HALF]
        return c

    flat[ROWS : ROWS + 24] = jnp.zeros((24, 128), F32)
    runs = [(0, 36), (36, 90), (90, 128)]
    swaps = []
    for m, (lo, hi) in enumerate(runs):
        grads(m)
        lax.fori_loop(lo // 2, hi // 2, lambda h, c: pack(2 * h + 1, pack(2 * h, c)), 0)
        part = pl.ds(lo, hi - lo)
        swaps.append(remote(pk.at[part], r0.at[part], dp_s, dp_r.at[m], partner))
        swaps[m].start()
    for m, (lo, hi) in enumerate(runs):
        swaps[m].wait_recv()
        lax.fori_loop(lo // 2, hi // 2, lambda h, c: merge(2 * h + 1, merge(2 * h, c)), 0)

    def mixed(k):
        return recvb[k].reshape(SLOTS, 128)

    def cat(ks):
        return jnp.concatenate([mixed(PLACE[k]) for k in ks], axis=1)

    message = {}

    def mix(m):
        if m == 0:
            zero = dot(cat(range(7)), w0[...]).astype(BF)
            for i in range(7):
                message[i] = zero[:, 128 * i : 128 * i + 128]
            return
        w = w1 if m == 1 else w2
        plus, length = GROUPS[2 * m - 1]
        minus = GROUPS[2 * m][0]
        p, q = cat(range(plus, plus + length)), cat(range(minus, minus + length))
        up = (dot(p, w[0]) - dot(q, w[1])).astype(BF)
        um = (dot(p, w[1]) + dot(q, w[0])).astype(BF)
        for i in range(length):
            message[plus + i] = up[:, 128 * i : 128 * i + 128]
            message[minus + i] = um[:, 128 * i : 128 * i + 128]

    def gather_atoms():
        for degree in range(LMAX + 1):
            w = width(degree)
            ks = [k for k in range(KEPT) if DEGREE[k] == degree]
            lhs = jnp.concatenate([leftd[k, :, 0:w] for k in ks], axis=0)
            rhs = jnp.concatenate([message[k] for k in ks], axis=0)
            got = lax.dot_general(lhs, rhs, (((0,), (0,)), ((), ())), preferred_element_type=F32)
            size = 2 * degree + 1
            agg[degree * degree : (degree + 1) * (degree + 1)] = (
                got[0 : ATOMS * size].astype(BF).reshape(size, ATOMS, 128)
            )

    def along_x(d):
        return at(lax.rem(x + d + NX, NX), z, y)

    def along_y(d):
        return at(x, z, lax.rem(y + d + NY, NY))

    def mod4(v):
        return lax.rem(v + 4, 4)

    parts = [(0, x, along_x, y, along_y), (1, y, along_y, x, along_x)]
    one, two, three, subs = [], [], [], []
    for i, p, move, q, _ in parts:
        order = [mod4(q + 2 * sign), mod4(q - sign), mod4(q + sign), q]
        subs.append(order)
        one.append(
            [remote(s0.at[i, mod4(p + 2 * sign), j], ra.at[i, j], st_s, st_r.at[i, n], move(sign))
             for n, j in enumerate(order)]
        )
        two.append(
            [remote(s0.at[i, mod4(p - sign), j], rb.at[i, j], st_s, st_r.at[i, 8], move(-sign))
             for n, j in enumerate(order)]
        )
        three.append(
            [remote(ta.at[i, j], rc.at[i, j], st_s, st_r.at[i, 4 + n], move(sign))
             for n, j in enumerate(order)]
        )
    def mod8(v):
        return lax.rem(v + 8, 8)

    def up(h, j):
        src = sz.at[mod8(z + 4 * sign), pl.ds(8 * j, 8)] if h == 0 else va.at[h - 1, j]
        return remote(src, ua.at[h, j], ua_s, ua_r.at[h, j], at(x, mod8(z + sign), y))

    def down(h, j):
        src = sz.at[mod8(z - 3 * sign), pl.ds(8 * j, 8)] if h == 0 else vb.at[h - 1, j]
        return remote(src, ub.at[h, j], ub_s, ub_r.at[h, j], at(x, mod8(z - sign), y))

    def pass_sum(h, j):
        part = pl.ds(8 * j, 8)
        up(h, j).wait_recv()
        va[h, j] = (ua[h, j].astype(F32) + sz[mod8(z + (3 - h) * sign), part].astype(F32)).astype(BF)
        up(h + 1, j).start()
        if h < 2:
            down(h, j).wait_recv()
            vb[h, j] = (ub[h, j].astype(F32) + sz[mod8(z - (2 - h) * sign), part].astype(F32)).astype(BF)
            down(h + 1, j).start()

    def end_sum(j):
        part = pl.ds(8 * j, 8)
        up(3, j).wait_recv()
        down(2, j).wait_recv()
        sz1[part] = (sz[z, part].astype(F32) + ua[3, j].astype(F32) + ub[2, j].astype(F32)).astype(BF)

    def relay(n):
        for i, p, *_ in parts:
            j = subs[i][n]
            one[i][n].wait_recv()
            ta[i, j] = (ra[i, j].astype(F32) + s0[i, mod4(p + sign), j].astype(F32)).astype(BF)
            three[i][n].start()

    four, five, six = [], [], []
    for i, p, _, q, move in parts:
        order = subs[i]
        four.append(remote(s1.at[i, order[0]], ra1.at[i], su_s, su_r.at[i, 0], move(sign)))
        five.append(remote(s1.at[i, order[1]], rb1.at[i], su_s, su_r.at[i, 1], move(-sign)))
        six.append(remote(ta1.at[i], rc1.at[i], su_s, su_r.at[i, 2], move(sign)))

    def close(n):
        for i, p, *_ in parts:
            j = subs[i][n]
            if n == 0:
                remote(rb.at[i], rb.at[i], st_s, st_r.at[i, 8], partner).wait_recv()
            three[i][n].wait_recv()
            s1[i, j] = (s0[i, p, j].astype(F32) + rb[i, j].astype(F32) + rc[i, j].astype(F32)).astype(BF)
            if n == 0:
                four[i].start()
            if n == 1:
                five[i].start()

    for j in range(2):
        up(0, j).start()
        down(0, j).start()
    for n in range(4):
        for i in range(2):
            one[i][n].start()
            two[i][n].start()
    for load in loads[3:]:
        load.wait()
    mix(1)
    mix(2)
    pass_sum(0, 0)
    relay(0)
    pass_sum(0, 1)
    relay(1)
    mix(0)
    pass_sum(1, 0)
    relay(2)
    pass_sum(1, 1)
    relay(3)
    pass_sum(2, 0)
    close(0)
    pass_sum(2, 1)
    for n in range(1, 4):
        close(n)
    for i in range(2):
        four[i].wait_recv()
        ta1[i] = (ra1[i].astype(F32) + s1[i, subs[i][2]].astype(F32)).astype(BF)
        six[i].start()
    for j in range(2):
        end_sum(j)

    def across(i):
        q = xypeer(i)
        return remote(sz1.at[q], r4.at[i], w_s, w_r, at(q // 4, z, q % 4))

    def across_go(h, c):
        for i in range(1, 6):
            across(5 * h + i).start()
        return c

    lax.fori_loop(0, 3, across_go, 0)
    def zcopy(a, i):
        q = zpeer(i)
        return remote(s2.at[a, q], r3.at[a, i], z_s, z_r.at[a], at(x, q, y))

    gather_atoms()
    store_agg = pltpu.make_async_copy(agg, agg_out, out_s.at[0])
    store_agg.start()
    for i in range(2):
        five[i].wait_recv()
        six[i].wait_recv()
        s2[i] = (s1[i, subs[i][3]].astype(F32) + rb1[i].astype(F32) + rc1[i].astype(F32)).astype(BF)
        for far in (4, 3, 5, 2, 6, 1, 7):
            zcopy(i, far).start()

    total = sz1[xy].astype(F32)
    part = r4.at[pl.ds(1, NXY - 1)]
    remote(part, part, w_s, w_r, partner).wait()
    for i in range(1, NXY):
        total = total + r4[i].astype(F32)
    fin[2 * RING : HALF] = total
    for a in range(2):
        total = s2[a, z].astype(F32)
        part = r3.at[a, pl.ds(1, NZ - 1)]
        remote(part, part, z_s, z_r.at[a], partner).wait_recv()
        for i in range(1, NZ):
            total = total + r3[a, i].astype(F32)
        fin[RING * a : RING * a + RING] = total
    mine = wgrad.at[pl.ds(pl.multiple_of(HALF * dp, 8), HALF)]
    last = remote(fin, mine, f_s, f_r, partner)
    last.start()
    store = pltpu.make_async_copy(fin, mine, out_s.at[1])
    store.start()
    for part, sem in (
        (ua, ua_s), (ub, ub_s), (s0.at[:, pl.ds(0, 3)], st_s), (s1.at[:, pl.ds(0, 3)], su_s),
        (s2.at[:, pl.ds(0, NZ - 1)], z_s), (pk, dp_s),
    ):
        remote(part, part, sem, f_r, partner).wait_send()
    gone = fall.at[pl.ds(0, 7), pl.ds(0, 784)]
    remote(gone, gone, ring_s, ring_r.at[0, 0], partner).wait_send()
    gone = sendb.at[:, :, pl.ds(0, NXY - 1)]
    remote(gone, gone, ex_s, ex_r.at[0], partner).wait_send()
    code_all(7, 0).wait_send()
    store_agg.wait()
    store.wait()
    last.wait()


def finish(agg_in, wgrad_in, agg, wgrad):
    agg[...] = agg_in[...]
    wgrad[...] = wgrad_in[0:SHARD]


def shards(features, cotangent, wigner, src_atom, dst_part, dst_atom, angle, w_zero, w_one, w_two):
    dma = pltpu.SemaphoreType.DMA
    scratch = [
        pltpu.VMEM((49, ATOMS, 128), BF),
        pltpu.VMEM((49, KEPT, 256), BF),
        pltpu.VMEM(w_zero.shape, BF),
        pltpu.VMEM(w_one.shape, BF),
        pltpu.VMEM(w_two.shape, BF),
        pltpu.VMEM((KEPT, SLOTS, 256), BF),
        pltpu.VMEM((KEPT, 64, 256), BF),
        pltpu.VMEM((KEPT, SLOTS, 256), BF),
        pltpu.VMEM((KEPT, SLOTS, 256), BF),
        pltpu.VMEM((NZ, 16, 128), BF),
        pltpu.VMEM((NZ, 3, 32, 128), BF),
        pltpu.VMEM((NZ, 832, 128), BF),
        pltpu.VMEM((832, 128), BF),
        pltpu.VMEM((NZ, WIRE, NXY, 2, 128), BF),
        pltpu.VMEM((WIRE, NZ, NXY, 2, 128), BF),
        pltpu.VMEM((KEPT, SLOTS, 128), BF),
        pltpu.VMEM((KEPT, 128, SLOTS), BF),
        pltpu.VMEM((ROWS + 24, 128), F32),
        pltpu.VMEM((128, HALF, 128), BF),
        pltpu.VMEM((128, HALF, 128), BF),
        pltpu.VMEM((2, 4, 4, NZ, RING, 128), BF),
    ]
    scratch += [pltpu.VMEM((2, 4, NZ, RING, 128), BF) for _ in range(4)]
    scratch += [pltpu.VMEM((2, 4, NZ, RING, 128), BF)]
    scratch += [pltpu.VMEM((2, NZ, RING, 128), BF) for _ in range(4)]
    scratch += [pltpu.VMEM((2, NZ, RING, 128), BF)]
    scratch += [
        pltpu.VMEM((2, NZ, RING, 128), BF),
        pltpu.VMEM((HALF, 128), F32),
        pltpu.VMEM((NZ, NXY, REST, 128), BF),
        pltpu.VMEM((4, 2, 8, REST, 128), BF),
        pltpu.VMEM((3, 2, 8, REST, 128), BF),
        pltpu.VMEM((3, 2, 8, REST, 128), BF),
        pltpu.VMEM((2, 2, 8, REST, 128), BF),
        pltpu.VMEM((NXY, REST, 128), BF),
        pltpu.VMEM((NXY, REST, 128), BF),
        dma, dma((3,)),
        dma, dma((7, 2)),
        dma, dma((2,)), dma((2,)),
        dma, dma((3,)),
        dma, dma((2, 9)),
        dma, dma((2, 3)),
        dma, dma((2,)),
        dma, dma,
        dma((6,)), dma((2,)),
        dma, dma((4, 2)), dma, dma((3, 2)), dma, dma,
    ]
    vmem = pl.BlockSpec(memory_space=pltpu.VMEM)
    agg, wgrad = pl.pallas_call(
        kernel,
        out_shape=(
            jax.ShapeDtypeStruct((49, ATOMS, 128), BF),
            jax.ShapeDtypeStruct((2 * HALF, 128), F32),
        ),
        in_specs=[vmem] * 4 + [pl.BlockSpec(memory_space=pl.ANY)] * 6,
        out_specs=(pl.BlockSpec(memory_space=pl.ANY),) * 2,
        scratch_shapes=scratch,
        compiler_params=pltpu.CompilerParams(
            collective_id=0, has_side_effects=True, vmem_limit_bytes=67000000
        ),
    )(
        dst_part.reshape(1, EDGES),
        src_atom.reshape(1, EDGES),
        dst_atom.reshape(1, EDGES),
        angle.reshape(1, EDGES),
        jnp.transpose(wigner, (2, 1, 0)),
        jnp.transpose(features, (1, 0, 2)).reshape(784, 128),
        jnp.transpose(cotangent, (1, 0, 2)).reshape(784, 128),
        w_zero, w_one, w_two,
    )
    agg, wgrad = pl.pallas_call(
        finish,
        out_shape=(
            jax.ShapeDtypeStruct((49, ATOMS, 128), BF),
            jax.ShapeDtypeStruct((SHARD, 128), F32),
        ),
        in_specs=[vmem] * 2,
        out_specs=(vmem, vmem),
    )(agg, wgrad)
    return jnp.transpose(agg, (1, 0, 2)), wgrad.reshape(SHARD * 128)


def solution(mesh):
    both = ("dp", "graph")
    placed = (
        P(both, None, None), P(both, None, None), P(), P(both), P(both, None), P(both), P(both), P(), P(), P(),
    )
    return jax.shard_map(
        shards,
        mesh=mesh,
        in_specs=placed,
        out_specs=(P(both, None, None), P("graph")),
        check_vma=False,
    )
```
